512 devices in a mesh: section: 8 (over y_lo, core), tile: 64 (over y_hi, x, z).
Axes of the slice: x: 4, y: 8 (y_hi: 2, y_lo: 4; y = y_hi * 4 + y_lo), z: 8, core: 2. Of those that a mesh axis runs over, the one named last changes fastest.
Arguments:
- frames: bfloat16 [4, 128, 64, 256], P(None, None, 'tile'), may hold values from -6 to 6
- weights: bfloat16 [8, 9, 512, 256], P('section'), may hold values from -0.375 to 0.375
- gate_bias: float32 [8, 512], P('section'), may hold values from -3 to 3
- cotangent: bfloat16 [8, 4, 128, 64, 256], P('section', None, None, 'tile'), may hold values from -6 to 6
Outputs:
- hidden_seq: bfloat16 [8, 4, 128, 64, 256], P('section', None, None, 'tile')
- input_grads: bfloat16 [8, 4, 128, 64, 256], P('section', None, None, 'tile')
The draws below stay inside these ranges and needn't reach their ends.
All inputs are finite; a program needn't handle non-finite values.
Results may differ from the reference program's by a relative error of at most 0.015.
Values may be sent and summed in bfloat16 or wider, within the bound.
A program may use at most 64 MiB of HBM per device.

```python
import jax
import jax.numpy as jnp
from jax import lax

CH = 128
STEPS = 4
TG = 8
TR = 16
TC = 16
LAYERS = 8
TILES = 64


def level_of(stream_key, shape, cuts, low, top_value):
    def one(axis_at, shards_of):
        heights = jax.random.uniform(jax.random.fold_in(jax.random.fold_in(stream_key, 6), axis_at), (shards_of,), jnp.float32, low / len(cuts), top_value / len(cuts))
        return jnp.repeat(jnp.exp(heights), shape[axis_at] // shards_of).reshape((-1,) + (1,) * (len(shape) - axis_at - 1))

    loudness = one(*cuts[0])
    for cut in cuts[1:]:
        loudness = loudness * one(*cut)
    return loudness


def noise(rng, dims, spread, reach, pieces=(), kind=jnp.bfloat16):
    drawn = spread * jax.random.normal(rng, dims, jnp.float32)
    if pieces:
        drawn = drawn * level_of(rng, dims, pieces, -0.22, 0.18)
    return jnp.clip(drawn, -reach, reach).astype(kind)


def setup_inputs(seed: int = 0) -> dict:
    keys = jax.random.split(jax.random.key(seed), 5)
    frames = noise(keys[0], (STEPS, CH, TILES, TR * TC), 1.0, 6.0, ((2, 64),))
    weights = noise(keys[1], (LAYERS, 9, 4 * CH, 2 * CH), (2 * CH) ** -0.5, 0.375, ((0, 8),))
    gate_bias = noise(keys[2], (LAYERS, 4 * CH), 0.5, 3.0, ((0, 8),), jnp.float32)
    cotangent = noise(keys[3], (LAYERS, STEPS, CH, TILES, TR * TC), 1.0, 6.0, ((0, 8), (3, 64)))
    return {"frames": frames, "weights": weights, "gate_bias": gate_bias, "cotangent": cotangent}


def to_grid(field):
    lead = field.shape[:-2]
    shaped = field.reshape(lead + (TILES // TG, TG, TR, TC))
    shaped = jnp.swapaxes(shaped, -3, -2)
    return shaped.reshape(lead + ((TILES // TG) * TR, TG * TC))


def to_tiles(field):
    lead = field.shape[:-2]
    shaped = field.reshape(lead + (TILES // TG, TR, TG, TC))
    shaped = jnp.swapaxes(shaped, -3, -2)
    return shaped.reshape(lead + (TILES, TR * TC))


def gate_terms(kernel, extended):
    padded = jnp.pad(extended, ((0, 0), (0, 0), (1, 1)))
    row_count = extended.shape[1] - 2
    col_count = extended.shape[2]
    summed = None
    for offset_row in range(3):
        for offset_col in range(3):
            window = padded[:, offset_row:offset_row + row_count, offset_col:offset_col + col_count]
            window = window.reshape(padded.shape[0], row_count * col_count)
            product_term = jnp.dot(kernel[offset_row * 3 + offset_col], window, preferred_element_type=jnp.float32)
            summed = product_term if summed is None else summed + product_term
    return summed.reshape(kernel.shape[1], row_count, col_count)


def input_terms(kernel, extended):
    padded = jnp.pad(extended, ((0, 0), (0, 0), (1, 1)))
    row_count = extended.shape[1] - 2
    col_count = extended.shape[2]
    summed = None
    for offset_row in range(3):
        for offset_col in range(3):
            window = padded[:, 2 - offset_row:2 - offset_row + row_count, 2 - offset_col:2 - offset_col + col_count]
            window = window.reshape(padded.shape[0], row_count * col_count)
            product_term = lax.dot_general(kernel[offset_row * 3 + offset_col], window, (((0,), (0,)), ((), ())), preferred_element_type=jnp.float32)
            summed = product_term if summed is None else summed + product_term
    return summed.reshape(kernel.shape[2], row_count, col_count)


def activate(preact):
    quarter = preact.shape[0] // 4
    return jnp.concatenate([jax.nn.sigmoid(preact[:2 * quarter]), jnp.tanh(preact[2 * quarter:3 * quarter]), jax.nn.sigmoid(preact[3 * quarter:])], 0)


def state_grads(gate_values, cell_prev, cell_now, d_hidden, d_cell):
    quarter = gate_values.shape[0] // 4
    in_gate = gate_values[:quarter]
    forget = gate_values[quarter:2 * quarter]
    cand_gate = gate_values[2 * quarter:3 * quarter]
    out_gate = gate_values[3 * quarter:]
    tanh_cell = jnp.tanh(cell_now)
    d_out = d_hidden * tanh_cell
    d_total = d_cell + d_hidden * out_gate * (1.0 - tanh_cell * tanh_cell)
    d_gates = jnp.concatenate([d_total * cand_gate * in_gate * (1.0 - in_gate), d_total * cell_prev * forget * (1.0 - forget), d_total * in_gate * (1.0 - cand_gate * cand_gate), d_out * out_gate * (1.0 - out_gate)], 0).astype(jnp.bfloat16)
    return d_gates, d_total * forget


def reference(frames, weights, gate_bias, cotangent):
    frames = to_grid(frames)
    cotangent = to_grid(cotangent)
    step_count = frames.shape[0]
    width_ch = frames.shape[1]
    plane = (width_ch, frames.shape[2], frames.shape[3])
    layer_inputs = [frames[step_index] for step_index in range(step_count)]
    hidden_layers = []
    gate_layers = []
    cell_layers = []
    for layer_index in range(LAYERS):
        hidden_now = jnp.zeros(plane, jnp.bfloat16)
        cell_now = jnp.zeros(plane, jnp.float32)
        hidden_list = []
        gate_list = []
        cell_list = [cell_now]
        for step_index in range(step_count):
            joined = jnp.concatenate([layer_inputs[step_index], hidden_now], 0)
            extended = jnp.pad(joined, ((0, 0), (1, 1), (0, 0)))
            gate_values = activate(gate_terms(weights[layer_index], extended) + gate_bias[layer_index][:, None, None])
            cell_now = gate_values[width_ch:2 * width_ch] * cell_now + gate_values[:width_ch] * gate_values[2 * width_ch:3 * width_ch]
            hidden_now = (gate_values[3 * width_ch:] * jnp.tanh(cell_now)).astype(jnp.bfloat16)
            hidden_list.append(hidden_now)
            gate_list.append(gate_values)
            cell_list.append(cell_now)
        hidden_layers.append(jnp.stack(hidden_list))
        gate_layers.append(gate_list)
        cell_layers.append(cell_list)
        layer_inputs = hidden_list
    from_above = [jnp.zeros(plane, jnp.float32) for step_index in range(step_count)]
    grad_layers = [None] * LAYERS
    for layer_index in reversed(range(LAYERS)):
        d_hidden_rec = jnp.zeros(plane, jnp.float32)
        d_cell = jnp.zeros(plane, jnp.float32)
        grad_list = [None] * step_count
        for step_index in reversed(range(step_count)):
            d_hidden = cotangent[layer_index, step_index].astype(jnp.float32) + from_above[step_index] + d_hidden_rec
            d_gates, d_cell = state_grads(gate_layers[layer_index][step_index], cell_layers[layer_index][step_index], cell_layers[layer_index][step_index + 1], d_hidden, d_cell)
            extended_grad = jnp.pad(d_gates, ((0, 0), (1, 1), (0, 0)))
            input_grad = input_terms(weights[layer_index], extended_grad)
            grad_list[step_index] = input_grad[:width_ch].astype(jnp.bfloat16)
            d_hidden_rec = input_grad[width_ch:]
        grad_layers[layer_index] = jnp.stack(grad_list)
        from_above = [grad_item.astype(jnp.float32) for grad_item in grad_list]
    return to_tiles(jnp.stack(hidden_layers)), to_tiles(jnp.stack(grad_layers))
```

```python
import jax
import jax.numpy as jnp
from jax import lax
from jax.experimental import pallas as pl
from jax.experimental.pallas import tpu as pltpu
from jax.sharding import PartitionSpec as P

TG = 8
TR = 16
TC = 16
CH = 128
STEPS = 4
PIX = TR * TC
EXT = (TR + 2) * TC
SLOTS = TR + 8
MESH = pl.DeviceIdType.MESH
BF = jnp.bfloat16
F32 = jnp.float32

SLOT_OF = {
    (-1, 0): 0,
    (1, 0): 17,
    (0, -1): 18,
    (0, 1): 19,
    (-1, -1): 20,
    (-1, 1): 21,
    (1, -1): 22,
    (1, 1): 23,
}


def kernel(
    sections,
    tiles,
    frames_ref,
    weights_ref,
    bias_ref,
    cot_ref,
    hidden_ref,
    grads_ref,
    xin,
    hin,
    dzin,
    din,
    hcol,
    dzcol,
    dsend,
    fcol,
    wf,
    wb,
    pick,
    edge,
    win_f,
    win_b,
    gates,
    cells,
    cot_t,
    x_sem,
    h_sem,
    dz_sem,
    d_sem,
    xs_sem,
    hs_sem,
    dzs_sem,
    ds_sem,
    w_sem,
):
    sec = lax.axis_index("section")
    tile = lax.axis_index("tile")
    grid_rows = tiles // TG
    row = lax.div(tile, TG)
    col = lax.rem(tile, TG)
    first = sec == 0
    last = sec == sections - 1

    def at(delta_row, delta_col):
        there_row = lax.rem(row + (delta_row + grid_rows), grid_rows)
        there_col = lax.rem(col + (delta_col + TG), TG)
        return there_row * TG + there_col

    copies = []
    for a in range(3):
        for b in range(3):
            copies.append(
                pltpu.make_async_copy(
                    weights_ref.at[3 * a + b], wf.at[a, :, pl.ds(2 * CH * b, 2 * CH)], w_sem.at[0, 3 * a + b]
                )
            )
            copies.append(
                pltpu.make_async_copy(
                    weights_ref.at[3 * a + 2 - b], wb.at[a, pl.ds(4 * CH * b, 4 * CH), :], w_sem.at[1, 3 * a + b]
                )
            )
    for copy in copies:
        copy.start()

    barrier = pltpu.get_barrier_semaphore()
    for delta in SLOT_OF:
        pl.semaphore_signal(barrier, inc=1, device_id={"section": sec, "tile": at(*delta)}, device_id_type=MESH)

    @pl.when(sec > 0)
    def _():
        for delta in SLOT_OF:
            pl.semaphore_signal(
                barrier, inc=1, device_id={"section": sec - 1, "tile": at(*delta)}, device_id_type=MESH
            )
        pl.semaphore_signal(barrier, inc=1, device_id={"section": sec - 1, "tile": tile}, device_id_type=MESH)

    @pl.when(sec < sections - 1)
    def _():
        pl.semaphore_signal(barrier, inc=1, device_id={"section": sec + 1, "tile": tile}, device_id_type=MESH)

    up_ok = row > 0
    down_ok = row < grid_rows - 1
    left_ok = col > 0
    right_ok = col < TG - 1
    out_at = lax.broadcasted_iota(jnp.int32, (EXT, SLOTS * TC), 0)
    src_at = lax.broadcasted_iota(jnp.int32, (EXT, SLOTS * TC), 1)
    r_at = lax.shift_right_logical(out_at, 4)
    q_at = lax.bitwise_and(out_at, TC - 1)
    bad_row = ((r_at == 0) & jnp.logical_not(up_ok)) | ((r_at == TR + 1) & jnp.logical_not(down_ok))
    for side in range(2):
        rim_q = 0 if side == 0 else TC - 1
        step = -1 if side == 0 else 1
        far = TC - 1 if side == 0 else 0
        side_ok = left_ok if side == 0 else right_ok
        rim_src = jnp.where(
            r_at == 0,
            (20 + side) * TC + far,
            jnp.where(r_at == TR + 1, (22 + side) * TC + far, (18 + side) * TC + r_at - 1),
        )
        on_rim = q_at == rim_q
        source = jnp.where(on_rim, rim_src, out_at + step)
        bad = bad_row | (on_rim & jnp.logical_not(side_ok))
        source = jnp.where(bad, -1, source)
        pick[side] = jnp.where(src_at == source, 1.0, 0.0).astype(BF)
    edge_out = lax.broadcasted_iota(jnp.int32, (2 * TR, PIX), 0)
    edge_src = lax.broadcasted_iota(jnp.int32, (2 * TR, PIX), 1)
    edge_want = jnp.where(edge_out < TR, edge_out * TC, (edge_out - TR) * TC + TC - 1)
    edge[...] = jnp.where(edge_src == edge_want, 1.0, 0.0).astype(BF)

    def columns(field):
        return jnp.dot(edge[...], field, preferred_element_type=F32).astype(BF)

    def rims(tile_buf, col_buf, dst, dst_t, section, send_sem, recv_sem):
        out = []
        for (delta_row, delta_col), slot in SLOT_OF.items():
            if delta_row == -1:
                piece = tile_buf.at[TR]
            elif delta_row == 1:
                piece = tile_buf.at[1]
            elif delta_col == -1:
                piece = col_buf.at[1]
            else:
                piece = col_buf.at[0]
            out.append(
                pltpu.make_async_remote_copy(
                    src_ref=piece,
                    dst_ref=dst.at[dst_t, slot],
                    send_sem=send_sem,
                    recv_sem=recv_sem,
                    device_id={"section": section, "tile": at(-delta_row, -delta_col)},
                    device_id_type=MESH,
                )
            )
        return out

    def wait_for(buf, sem):
        pltpu.make_async_copy(buf, buf, sem).wait()

    def turn_cotangent():
        def turn(t, carry):
            cot_t[t] = cot_ref[t].astype(F32).T
            return carry

        lax.fori_loop(0, STEPS, turn, 0)

    hin[0] = jnp.zeros((SLOTS, TC, CH), BF)

    @pl.when(first)
    def _():
        def place(t, carry):
            field = frames_ref[t].astype(F32).T.astype(BF)
            xin[t, 1 : TR + 1] = field.reshape(TR, TC, CH)
            fcol[t] = columns(field).reshape(2, TR, CH)
            return carry

        lax.fori_loop(0, STEPS, place, 0)

    @pl.when(sec > 0)
    def _():
        turn_cotangent()

    pl.semaphore_wait(
        barrier,
        8 + jnp.where(last, 0, 9) + jnp.where(first, 0, 1),
    )

    @pl.when(first)
    def _():
        def share(t, carry):
            for copy in rims(xin.at[t], fcol.at[t], xin, t, sec, xs_sem.at[t], x_sem.at[t]):
                copy.start()
            return carry

        lax.fori_loop(0, STEPS, share, 0)

    for copy in copies[0::2]:
        copy.wait()

    up_f = jnp.where(up_ok, 1.0, 0.0)
    down_f = jnp.where(down_ok, 1.0, 0.0)

    def middle(buf, t, width):
        top = (buf[t, 0].astype(F32) * up_f).astype(BF)
        low = (buf[t, TR + 1].astype(F32) * down_f).astype(BF)
        return top, buf[t, 1 : TR + 1].reshape(PIX, width), low

    def spread(buf, t, width, win, base, stride):
        whole = buf[t].reshape(SLOTS * TC, width)
        for side in range(2):
            moved = jnp.dot(pick[side], whole, preferred_element_type=F32).astype(BF)
            win[:, pl.ds(2 * side * stride + base, width)] = moved
        top, mid, low = middle(buf, t, width)
        win[0:TC, pl.ds(stride + base, width)] = top
        win[TC : TC + PIX, pl.ds(stride + base, width)] = mid
        win[TC + PIX : EXT, pl.ds(stride + base, width)] = low

    cells[0] = jnp.zeros((PIX, CH), F32)

    def forward(t, carry):
        @pl.when(t > 0)
        def _():
            wait_for(hin.at[t, pl.ds(0, 8)], h_sem.at[t])

        spread(hin, t, CH, win_f, CH, 2 * CH)

        @pl.when(first)
        def _():
            wait_for(xin.at[t, pl.ds(0, 8)], x_sem.at[t])

        @pl.when(sec > 0)
        def _():
            wait_for(xin.at[t], x_sem.at[t])

        spread(xin, t, CH, win_f, 0, 2 * CH)
        z = bias_ref[...]
        for a in range(3):
            z = z + lax.dot_general(
                win_f[a * TC : a * TC + PIX, :],
                wf[a],
                (((1,), (1,)), ((), ())),
                preferred_element_type=F32,
            )
        in_gate = jax.nn.sigmoid(z[:, :CH])
        forget = jax.nn.sigmoid(z[:, CH : 2 * CH])
        cand = jnp.tanh(z[:, 2 * CH : 3 * CH])
        out_gate = jax.nn.sigmoid(z[:, 3 * CH :])
        cell = forget * cells[t] + in_gate * cand
        hidden = out_gate * jnp.tanh(cell)
        field = hidden.astype(BF)
        hin[t + 1, 1 : TR + 1] = field.reshape(TR, TC, CH)
        hcol[t] = columns(field).reshape(2, TR, CH)

        @pl.when(sec < sections - 1)
        def _():
            pltpu.make_async_remote_copy(
                src_ref=hin.at[t + 1, pl.ds(1, TR)],
                dst_ref=xin.at[t, pl.ds(1, TR)],
                send_sem=xs_sem.at[STEPS + t],
                recv_sem=x_sem.at[t],
                device_id={"section": sec + 1, "tile": tile},
                device_id_type=MESH,
            ).start()
            for copy in rims(hin.at[t + 1], hcol.at[t], xin, t, sec + 1, xs_sem.at[STEPS + t], x_sem.at[t]):
                copy.start()

        @pl.when(t < STEPS - 1)
        def _():
            for copy in rims(hin.at[t + 1], hcol.at[t], hin, t + 1, sec, hs_sem.at[t], h_sem.at[t + 1]):
                copy.start()

        gates[t, :, 0:CH] = in_gate
        gates[t, :, CH : 2 * CH] = forget
        gates[t, :, 2 * CH : 3 * CH] = cand
        gates[t, :, 3 * CH :] = out_gate
        cells[t + 1] = cell
        hidden_ref[t] = hidden.T.astype(BF)
        return carry

    lax.fori_loop(0, STEPS, forward, 0)

    @pl.when(first)
    def _():
        turn_cotangent()

    for copy in copies[1::2]:
        copy.wait()

    def backward(back, carry):
        d_rec, d_cell = carry
        t = STEPS - 1 - back

        @pl.when(sec < sections - 1)
        def _():
            wait_for(din.at[t], d_sem.at[t])

        in_gate = gates[t, :, 0:CH]
        forget = gates[t, :, CH : 2 * CH]
        cand = gates[t, :, 2 * CH : 3 * CH]
        out_gate = gates[t, :, 3 * CH :]
        tanh_cell = jnp.tanh(cells[t + 1])
        d_hidden = cot_t[t] + din[t].astype(F32) + d_rec
        d_total = d_cell + d_hidden * out_gate * (1.0 - tanh_cell * tanh_cell)
        parts = [
            d_total * cand * in_gate * (1.0 - in_gate),
            d_total * cells[t] * forget * (1.0 - forget),
            d_total * in_gate * (1.0 - cand * cand),
            d_hidden * tanh_cell * out_gate * (1.0 - out_gate),
        ]
        dz = jnp.concatenate([part.astype(BF) for part in parts], 1)
        dzin[t, 1 : TR + 1] = dz.reshape(TR, TC, 4 * CH)
        dzcol[t] = columns(dz).reshape(2, TR, 4 * CH)
        for copy in rims(dzin.at[t], dzcol.at[t], dzin, t, sec, dzs_sem.at[t], dz_sem.at[t]):
            copy.start()
        wait_for(dzin.at[t, pl.ds(0, 8)], dz_sem.at[t])
        spread(dzin, t, 4 * CH, win_b, 0, 4 * CH)
        du = None
        for a in range(3):
            term = jnp.dot(
                win_b[(2 - a) * TC : (2 - a) * TC + PIX, :], wb[a], preferred_element_type=F32
            )
            du = term if du is None else du + term
        d_input = du[:, :CH]
        dsend[t] = d_input.astype(BF)

        @pl.when(sec > 0)
        def _():
            pltpu.make_async_remote_copy(
                src_ref=dsend.at[t],
                dst_ref=din.at[t],
                send_sem=ds_sem.at[t],
                recv_sem=d_sem.at[t],
                device_id={"section": sec - 1, "tile": tile},
                device_id_type=MESH,
            ).start()

        grads_ref[t] = d_input.T.astype(BF)
        return du[:, CH:], d_total * forget

    @pl.when(last)
    def _():
        din[...] = jnp.zeros(din.shape, BF)

    zero = jnp.zeros((PIX, CH), F32)
    lax.fori_loop(0, STEPS, backward, (zero, zero))

    def settle(t, carry):
        @pl.when(first)
        def _():
            wait_for(xin.at[t, pl.ds(0, 8)], xs_sem.at[t])

        @pl.when(sec < sections - 1)
        def _():
            wait_for(xin.at[t], xs_sem.at[STEPS + t])

        @pl.when(t < STEPS - 1)
        def _():
            wait_for(hin.at[t, pl.ds(0, 8)], hs_sem.at[t])

        wait_for(dzin.at[t, pl.ds(0, 8)], dzs_sem.at[t])

        @pl.when(sec > 0)
        def _():
            wait_for(dsend.at[t], ds_sem.at[t])

        return carry

    lax.fori_loop(0, STEPS, settle, 0)


def make_step(sections, tiles):
    def body(*refs):
        kernel(sections, tiles, *refs)

    return pl.pallas_call(
        body,
        out_shape=[jax.ShapeDtypeStruct((STEPS, CH, PIX), BF)] * 2,
        in_specs=[
            pl.BlockSpec(memory_space=pltpu.VMEM),
            pl.BlockSpec(memory_space=pl.ANY),
            pl.BlockSpec(memory_space=pltpu.VMEM),
            pl.BlockSpec(memory_space=pltpu.VMEM),
        ],
        out_specs=[pl.BlockSpec(memory_space=pltpu.VMEM)] * 2,
        scratch_shapes=[
            pltpu.VMEM((STEPS, SLOTS, TC, CH), BF),
            pltpu.VMEM((STEPS + 1, SLOTS, TC, CH), BF),
            pltpu.VMEM((STEPS, SLOTS, TC, 4 * CH), BF),
            pltpu.VMEM((STEPS, PIX, CH), BF),
            pltpu.VMEM((STEPS, 2, TR, CH), BF),
            pltpu.VMEM((STEPS, 2, TR, 4 * CH), BF),
            pltpu.VMEM((STEPS, PIX, CH), BF),
            pltpu.VMEM((STEPS, 2, TR, CH), BF),
            pltpu.VMEM((3, 4 * CH, 6 * CH), BF),
            pltpu.VMEM((3, 12 * CH, 2 * CH), BF),
            pltpu.VMEM((2, EXT, SLOTS * TC), BF),
            pltpu.VMEM((2 * TR, PIX), BF),
            pltpu.VMEM((EXT, 6 * CH), BF),
            pltpu.VMEM((EXT, 12 * CH), BF),
            pltpu.VMEM((STEPS, PIX, 4 * CH), F32),
            pltpu.VMEM((STEPS + 1, PIX, CH), F32),
            pltpu.VMEM((STEPS, PIX, CH), F32),
            pltpu.SemaphoreType.DMA((STEPS,)),
            pltpu.SemaphoreType.DMA((STEPS,)),
            pltpu.SemaphoreType.DMA((STEPS,)),
            pltpu.SemaphoreType.DMA((STEPS,)),
            pltpu.SemaphoreType.DMA((2 * STEPS,)),
            pltpu.SemaphoreType.DMA((STEPS,)),
            pltpu.SemaphoreType.DMA((STEPS,)),
            pltpu.SemaphoreType.DMA((STEPS,)),
            pltpu.SemaphoreType.DMA((2, 9)),
        ],
        compiler_params=pltpu.CompilerParams(
            collective_id=0, has_side_effects=True, vmem_limit_bytes=56 * 1024 * 1024
        ),
        name="conv_lstm",
    )


def solution(mesh):
    step = make_step(mesh.shape["section"], mesh.shape["tile"])

    def per_device(frames, weights, gate_bias, cotangent):
        hidden, grads = step(
            frames.reshape(STEPS, CH, PIX), weights[0], gate_bias, cotangent.reshape(STEPS, CH, PIX)
        )
        shape = (1, STEPS, CH, 1, PIX)
        return hidden.reshape(shape), grads.reshape(shape)

    in_specs = (
        P(None, None, "tile", None),
        P("section", None, None, None),
        P("section", None),
        P("section", None, None, "tile", None),
    )
    out_specs = (P("section", None, None, "tile", None), P("section", None, None, "tile", None))
    return jax.shard_map(
        per_device, mesh=mesh, in_specs=in_specs, out_specs=out_specs, check_vma=False
    )
```

```python
import jax
import jax.numpy as jnp
from jax import lax
from jax.experimental import pallas as pl
from jax.experimental.pallas import tpu as pltpu
from jax.sharding import PartitionSpec as P

TG = 8
TR = 16
TC = 16
CH = 128
STEPS = 4
PIX = TR * TC
EXT = (TR + 2) * TC
SLOTS = TR + 8
MESH = pl.DeviceIdType.MESH
BF = jnp.bfloat16
F32 = jnp.float32

NEAR = TR + 2
FAR = 6
FAR_SLOTS = {
    (-1, 0): 18,
    (1, 0): 19,
    (-1, -1): 20,
    (-1, 1): 21,
    (1, -1): 22,
    (1, 1): 23,
}
NEAR_SLOTS = {(0, -1): 16, (0, 1): 17}
SLOT_OF = {**FAR_SLOTS, **NEAR_SLOTS}


def kernel(
    sections,
    tiles,
    frames_ref,
    weights_ref,
    bias_ref,
    cot_ref,
    hidden_ref,
    grads_ref,
    xin,
    hin,
    dzin,
    din,
    hcol,
    dzcol,
    dsend,
    fcol,
    wf,
    wb,
    pick,
    pick_far,
    edge,
    win_f,
    win_b,
    far_f,
    far_b,
    z_ref,
    du_ref,
    dc_ref,
    gates,
    cells,
    cot_t,
    x_sem,
    h_sem,
    dz_sem,
    d_sem,
    xs_sem,
    hs_sem,
    dzs_sem,
    ds_sem,
    w_sem,
):
    sec = lax.axis_index("section")
    tile = lax.axis_index("tile")
    grid_rows = tiles // TG
    row = lax.div(tile, TG)
    col = lax.rem(tile, TG)
    first = sec == 0
    last = sec == sections - 1

    def at(delta_row, delta_col):
        there_row = lax.rem(row + (delta_row + grid_rows), grid_rows)
        there_col = lax.rem(col + (delta_col + TG), TG)
        return there_row * TG + there_col

    copies = []
    for a in range(3):
        for b in range(3):
            copies.append(
                pltpu.make_async_copy(
                    weights_ref.at[3 * a + b], wf.at[a, :, pl.ds(2 * CH * b, 2 * CH)], w_sem.at[0, 3 * a + b]
                )
            )
            copies.append(
                pltpu.make_async_copy(
                    weights_ref.at[3 * a + 2 - b], wb.at[a, pl.ds(4 * CH * b, 4 * CH), :], w_sem.at[1, 3 * a + b]
                )
            )
    for copy in copies:
        copy.start()

    barrier = pltpu.get_barrier_semaphore()
    for delta in SLOT_OF:
        pl.semaphore_signal(barrier, inc=1, device_id={"section": sec, "tile": at(*delta)}, device_id_type=MESH)

    @pl.when(sec > 0)
    def _():
        for delta in SLOT_OF:
            pl.semaphore_signal(
                barrier, inc=1, device_id={"section": sec - 1, "tile": at(*delta)}, device_id_type=MESH
            )
        pl.semaphore_signal(barrier, inc=1, device_id={"section": sec - 1, "tile": tile}, device_id_type=MESH)

    @pl.when(sec < sections - 1)
    def _():
        pl.semaphore_signal(barrier, inc=1, device_id={"section": sec + 1, "tile": tile}, device_id_type=MESH)

    up_ok = row > 0
    down_ok = row < grid_rows - 1
    left_ok = col > 0
    right_ok = col < TG - 1
    out_at = lax.broadcasted_iota(jnp.int32, (PIX, NEAR * TC), 0)
    src_at = lax.broadcasted_iota(jnp.int32, (PIX, NEAR * TC), 1)
    r_at = lax.shift_right_logical(out_at, 4)
    q_at = lax.bitwise_and(out_at, TC - 1)
    for side in range(2):
        side_ok = left_ok if side == 0 else right_ok
        on_rim = q_at == (0 if side == 0 else TC - 1)
        source = jnp.where(on_rim, (TR + side) * TC + r_at, out_at + (2 * side - 1))
        source = jnp.where(on_rim & jnp.logical_not(side_ok), -1, source)
        pick[side] = jnp.where(src_at == source, 1.0, 0.0).astype(BF)
    out_at = lax.broadcasted_iota(jnp.int32, (2 * TC, FAR * TC), 0)
    src_at = lax.broadcasted_iota(jnp.int32, (2 * TC, FAR * TC), 1)
    low = lax.shift_right_logical(out_at, 4)
    q_at = lax.bitwise_and(out_at, TC - 1)
    bad_row = ((low == 0) & jnp.logical_not(up_ok)) | ((low == 1) & jnp.logical_not(down_ok))
    for b in range(3):
        q_src = q_at + (b - 1)
        over_left = q_src < 0
        over_right = q_src >= TC
        source = jnp.where(
            over_left,
            (2 + 2 * low) * TC + TC - 1,
            jnp.where(over_right, (3 + 2 * low) * TC, low * TC + q_src),
        )
        bad = bad_row | (over_left & jnp.logical_not(left_ok)) | (over_right & jnp.logical_not(right_ok))
        source = jnp.where(bad, -1, source)
        pick_far[b] = jnp.where(src_at == source, 1.0, 0.0).astype(BF)
    edge_out = lax.broadcasted_iota(jnp.int32, (2 * TR, PIX), 0)
    edge_src = lax.broadcasted_iota(jnp.int32, (2 * TR, PIX), 1)
    edge_want = jnp.where(edge_out < TR, edge_out * TC, (edge_out - TR) * TC + TC - 1)
    edge[...] = jnp.where(edge_src == edge_want, 1.0, 0.0).astype(BF)

    def columns(field):
        return jnp.dot(edge[...], field, preferred_element_type=F32).astype(BF)

    def rims(slots, tile_buf, col_buf, dst, dst_t, section, send_sem, recv_sem):
        for (delta_row, delta_col), slot in slots.items():
            if delta_row == -1:
                piece = tile_buf.at[TR - 1]
            elif delta_row == 1:
                piece = tile_buf.at[0]
            elif delta_col == -1:
                piece = col_buf.at[1]
            else:
                piece = col_buf.at[0]
            pltpu.make_async_remote_copy(
                src_ref=piece,
                dst_ref=dst.at[dst_t, slot],
                send_sem=send_sem,
                recv_sem=recv_sem,
                device_id={"section": section, "tile": at(-delta_row, -delta_col)},
                device_id_type=MESH,
            ).start()

    def wait_for(buf, sem):
        pltpu.make_async_copy(buf, buf, sem).wait()

    def turn_cotangent():
        def turn(t, carry):
            cot_t[t] = cot_ref[t].astype(F32).T
            return carry

        lax.fori_loop(0, STEPS, turn, 0)

    hin[0] = jnp.zeros((SLOTS, TC, CH), BF)
    for win in (win_f, win_b):
        rim = jnp.zeros((TC, win.shape[1]), BF)
        win[0:TC, :] = rim
        win[TC + PIX : EXT, :] = rim

    @pl.when(first)
    def _():
        def place(t, carry):
            field = frames_ref[t].astype(F32).T.astype(BF)
            xin[t, 0:TR] = field.reshape(TR, TC, CH)
            fcol[t] = columns(field).reshape(2, TR, CH)
            return carry

        lax.fori_loop(0, STEPS, place, 0)

    @pl.when(sec > 0)
    def _():
        turn_cotangent()

    pl.semaphore_wait(
        barrier,
        8 + jnp.where(last, 0, 9) + jnp.where(first, 0, 1),
    )

    @pl.when(first)
    def _():
        def share(t, carry):
            rims(FAR_SLOTS, xin.at[t], fcol.at[t], xin, t, sec, xs_sem.at[t], x_sem.at[STEPS + t])
            rims(NEAR_SLOTS, xin.at[t], fcol.at[t], xin, t, sec, xs_sem.at[t], x_sem.at[t])
            return carry

        lax.fori_loop(0, STEPS, share, 0)

    for copy in copies[0::2]:
        copy.wait()

    def spread(buf, t, width, win, base, stride):
        whole = buf[t, 0:NEAR].reshape(NEAR * TC, width)
        for side in range(2):
            moved = jnp.dot(pick[side], whole, preferred_element_type=F32).astype(BF)
            win[TC : TC + PIX, pl.ds(2 * side * stride + base, width)] = moved
        win[TC : TC + PIX, pl.ds(stride + base, width)] = whole[:PIX]

    def spread_far(buf, t, width, win, base, stride):
        whole = buf[t, NEAR:SLOTS].reshape(FAR * TC, width)
        for b in range(3):
            moved = jnp.dot(pick_far[b], whole, preferred_element_type=F32).astype(BF)
            win[:, pl.ds(b * stride + base, width)] = moved

    cells[0] = jnp.zeros((PIX, CH), F32)

    def send_rows(buf, buf_t, dst, dst_t, start, count, section, send_sem, recv_sem):
        pltpu.make_async_remote_copy(
            src_ref=buf.at[buf_t, pl.ds(start, count)],
            dst_ref=dst.at[dst_t, pl.ds(start, count)],
            send_sem=send_sem,
            recv_sem=recv_sem,
            device_id={"section": section, "tile": tile},
            device_id_type=MESH,
        ).start()

    def advance(t, low, high):
        z = z_ref[low:high, :]
        in_gate = jax.nn.sigmoid(z[:, :CH])
        forget = jax.nn.sigmoid(z[:, CH : 2 * CH])
        cand = jnp.tanh(z[:, 2 * CH : 3 * CH])
        out_gate = jax.nn.sigmoid(z[:, 3 * CH :])
        cell = forget * cells[t, low:high, :] + in_gate * cand
        hidden = (out_gate * jnp.tanh(cell)).astype(BF)
        hin[t + 1, low // TC : high // TC] = hidden.reshape((high - low) // TC, TC, CH)
        gates[t, low:high, 0:CH] = in_gate
        gates[t, low:high, CH : 2 * CH] = forget
        gates[t, low:high, 2 * CH : 3 * CH] = cand
        gates[t, low:high, 3 * CH :] = out_gate
        cells[t + 1, low:high, :] = cell

    def forward(t, carry):
        @pl.when(t > 0)
        def _():
            wait_for(hin.at[t, pl.ds(TR, 2)], h_sem.at[t])

        spread(hin, t, CH, win_f, CH, 2 * CH)

        @pl.when(first)
        def _():
            wait_for(xin.at[t, pl.ds(TR, 2)], x_sem.at[t])

        @pl.when(sec > 0)
        def _():
            wait_for(xin.at[t, pl.ds(0, NEAR)], x_sem.at[t])

        spread(xin, t, CH, win_f, 0, 2 * CH)
        z = bias_ref[...]
        for a in range(3):
            z = z + lax.dot_general(
                win_f[a * TC : a * TC + PIX, :],
                wf[a],
                (((1,), (1,)), ((), ())),
                preferred_element_type=F32,
            )
        z_ref[...] = z
        advance(t, TC, PIX - TC)

        @pl.when(sec < sections - 1)
        def _():
            send_rows(hin, t + 1, xin, t, 1, TR - 2, sec + 1, xs_sem.at[STEPS + t], x_sem.at[t])

        @pl.when(t > 0)
        def _():
            wait_for(hin.at[t, pl.ds(NEAR, FAR)], h_sem.at[STEPS + t])

        wait_for(xin.at[t, pl.ds(NEAR, FAR)], x_sem.at[STEPS + t])
        spread_far(hin, t, CH, far_f, CH, 2 * CH)
        spread_far(xin, t, CH, far_f, 0, 2 * CH)
        for a, start in ((0, 0), (2, PIX - TC)):
            far = far_f[0:TC, :] if a == 0 else far_f[TC : 2 * TC, :]
            z_ref[start : start + TC, :] += lax.dot_general(
                far, wf[a], (((1,), (1,)), ((), ())), preferred_element_type=F32
            )
        advance(t, 0, TC)
        advance(t, PIX - TC, PIX)

        @pl.when(sec < sections - 1)
        def _():
            rims(FAR_SLOTS, hin.at[t + 1], hcol.at[t], xin, t, sec + 1, xs_sem.at[STEPS + t], x_sem.at[STEPS + t])
            for edge_row in (0, TR - 1):
                send_rows(hin, t + 1, xin, t, edge_row, 1, sec + 1, xs_sem.at[STEPS + t], x_sem.at[t])

        @pl.when(t < STEPS - 1)
        def _():
            rims(FAR_SLOTS, hin.at[t + 1], hcol.at[t], hin, t + 1, sec, hs_sem.at[t], h_sem.at[STEPS + t + 1])

        field = hin[t + 1, 0:TR].reshape(PIX, CH)
        hcol[t] = columns(field).reshape(2, TR, CH)

        @pl.when(sec < sections - 1)
        def _():
            rims(NEAR_SLOTS, hin.at[t + 1], hcol.at[t], xin, t, sec + 1, xs_sem.at[STEPS + t], x_sem.at[t])

        @pl.when(t < STEPS - 1)
        def _():
            rims(NEAR_SLOTS, hin.at[t + 1], hcol.at[t], hin, t + 1, sec, hs_sem.at[t], h_sem.at[t + 1])

        hidden_ref[t] = field.astype(F32).T.astype(BF)
        return carry

    lax.fori_loop(0, STEPS, forward, 0)

    @pl.when(first)
    def _():
        turn_cotangent()

    for copy in copies[1::2]:
        copy.wait()

    def backward(back, carry):
        t = STEPS - 1 - back

        @pl.when(sec < sections - 1)
        def _():
            wait_for(din.at[t], d_sem.at[t])

        in_gate = gates[t, :, 0:CH]
        forget = gates[t, :, CH : 2 * CH]
        cand = gates[t, :, 2 * CH : 3 * CH]
        out_gate = gates[t, :, 3 * CH :]
        tanh_cell = jnp.tanh(cells[t + 1])
        d_hidden = cot_t[t] + din[t].reshape(PIX, CH).astype(F32) + du_ref[:, CH:]
        d_total = dc_ref[...] + d_hidden * out_gate * (1.0 - tanh_cell * tanh_cell)
        parts = [
            d_total * cand * in_gate * (1.0 - in_gate),
            d_total * cells[t] * forget * (1.0 - forget),
            d_total * in_gate * (1.0 - cand * cand),
            d_hidden * tanh_cell * out_gate * (1.0 - out_gate),
        ]
        dz = jnp.concatenate([part.astype(BF) for part in parts], 1)
        dc_ref[...] = d_total * forget
        dzin[t, 0:TR] = dz.reshape(TR, TC, 4 * CH)
        rims(FAR_SLOTS, dzin.at[t], dzcol.at[t], dzin, t, sec, dzs_sem.at[t], dz_sem.at[STEPS + t])
        dzcol[t] = columns(dz).reshape(2, TR, 4 * CH)
        rims(NEAR_SLOTS, dzin.at[t], dzcol.at[t], dzin, t, sec, dzs_sem.at[t], dz_sem.at[t])
        wait_for(dzin.at[t, pl.ds(TR, 2)], dz_sem.at[t])
        spread(dzin, t, 4 * CH, win_b, 0, 4 * CH)
        du = None
        for a in range(3):
            term = jnp.dot(
                win_b[(2 - a) * TC : (2 - a) * TC + PIX, :], wb[a], preferred_element_type=F32
            )
            du = term if du is None else du + term
        du_ref[...] = du
        dsend[t] = du[:, :CH].astype(BF).reshape(TR, TC, CH)
        above = (dsend, t, din, t)

        @pl.when(sec > 0)
        def _():
            send_rows(*above, 1, TR - 2, sec - 1, ds_sem.at[t], d_sem.at[t])

        wait_for(dzin.at[t, pl.ds(NEAR, FAR)], dz_sem.at[STEPS + t])
        spread_far(dzin, t, 4 * CH, far_b, 0, 4 * CH)
        for a, start in ((2, 0), (0, PIX - TC)):
            far = far_b[0:TC, :] if a == 2 else far_b[TC : 2 * TC, :]
            rim = du_ref[start : start + TC, :] + jnp.dot(far, wb[a], preferred_element_type=F32)
            du_ref[start : start + TC, :] = rim
            dsend[t, start // TC] = rim[:, :CH].astype(BF)

        @pl.when(sec > 0)
        def _():
            for edge_row in (0, TR - 1):
                send_rows(*above, edge_row, 1, sec - 1, ds_sem.at[t], d_sem.at[t])

        grads_ref[t] = du_ref[:, :CH].T.astype(BF)
        return carry

    @pl.when(last)
    def _():
        din[...] = jnp.zeros(din.shape, BF)

    du_ref[...] = jnp.zeros(du_ref.shape, F32)
    dc_ref[...] = jnp.zeros(dc_ref.shape, F32)
    lax.fori_loop(0, STEPS, backward, 0)

    def settle(t, carry):
        @pl.when(first)
        def _():
            wait_for(xin.at[t, pl.ds(0, 8)], xs_sem.at[t])

        @pl.when(sec < sections - 1)
        def _():
            wait_for(xin.at[t], xs_sem.at[STEPS + t])

        @pl.when(t < STEPS - 1)
        def _():
            wait_for(hin.at[t, pl.ds(0, 8)], hs_sem.at[t])

        wait_for(dzin.at[t, pl.ds(0, 8)], dzs_sem.at[t])

        @pl.when(sec > 0)
        def _():
            wait_for(dsend.at[t], ds_sem.at[t])

        return carry

    lax.fori_loop(0, STEPS, settle, 0)


def make_step(sections, tiles):
    def body(*refs):
        kernel(sections, tiles, *refs)

    return pl.pallas_call(
        body,
        out_shape=[jax.ShapeDtypeStruct((STEPS, CH, PIX), BF)] * 2,
        in_specs=[
            pl.BlockSpec(memory_space=pltpu.VMEM),
            pl.BlockSpec(memory_space=pl.ANY),
            pl.BlockSpec(memory_space=pltpu.VMEM),
            pl.BlockSpec(memory_space=pltpu.VMEM),
        ],
        out_specs=[pl.BlockSpec(memory_space=pltpu.VMEM)] * 2,
        scratch_shapes=[
            pltpu.VMEM((STEPS, SLOTS, TC, CH), BF),
            pltpu.VMEM((STEPS + 1, SLOTS, TC, CH), BF),
            pltpu.VMEM((STEPS, SLOTS, TC, 4 * CH), BF),
            pltpu.VMEM((STEPS, TR, TC, CH), BF),
            pltpu.VMEM((STEPS, 2, TR, CH), BF),
            pltpu.VMEM((STEPS, 2, TR, 4 * CH), BF),
            pltpu.VMEM((STEPS, TR, TC, CH), BF),
            pltpu.VMEM((STEPS, 2, TR, CH), BF),
            pltpu.VMEM((3, 4 * CH, 6 * CH), BF),
            pltpu.VMEM((3, 12 * CH, 2 * CH), BF),
            pltpu.VMEM((2, PIX, NEAR * TC), BF),
            pltpu.VMEM((3, 2 * TC, FAR * TC), BF),
            pltpu.VMEM((2 * TR, PIX), BF),
            pltpu.VMEM((EXT, 6 * CH), BF),
            pltpu.VMEM((EXT, 12 * CH), BF),
            pltpu.VMEM((2 * TC, 6 * CH), BF),
            pltpu.VMEM((2 * TC, 12 * CH), BF),
            pltpu.VMEM((PIX, 4 * CH), F32),
            pltpu.VMEM((PIX, 2 * CH), F32),
            pltpu.VMEM((PIX, CH), F32),
            pltpu.VMEM((STEPS, PIX, 4 * CH), F32),
            pltpu.VMEM((STEPS + 1, PIX, CH), F32),
            pltpu.VMEM((STEPS, PIX, CH), F32),
            pltpu.SemaphoreType.DMA((2 * STEPS,)),
            pltpu.SemaphoreType.DMA((2 * STEPS,)),
            pltpu.SemaphoreType.DMA((2 * STEPS,)),
            pltpu.SemaphoreType.DMA((STEPS,)),
            pltpu.SemaphoreType.DMA((2 * STEPS,)),
            pltpu.SemaphoreType.DMA((STEPS,)),
            pltpu.SemaphoreType.DMA((STEPS,)),
            pltpu.SemaphoreType.DMA((STEPS,)),
            pltpu.SemaphoreType.DMA((2, 9)),
        ],
        compiler_params=pltpu.CompilerParams(
            collective_id=0, has_side_effects=True, vmem_limit_bytes=56 * 1024 * 1024
        ),
        name="conv_lstm",
    )


def solution(mesh):
    step = make_step(mesh.shape["section"], mesh.shape["tile"])

    def per_device(frames, weights, gate_bias, cotangent):
        hidden, grads = step(
            frames.reshape(STEPS, CH, PIX), weights[0], gate_bias, cotangent.reshape(STEPS, CH, PIX)
        )
        shape = (1, STEPS, CH, 1, PIX)
        return hidden.reshape(shape), grads.reshape(shape)

    in_specs = (
        P(None, None, "tile", None),
        P("section", None, None, None),
        P("section", None),
        P("section", None, None, "tile", None),
    )
    out_specs = (P("section", None, None, "tile", None), P("section", None, None, "tile", None))
    return jax.shard_map(
        per_device, mesh=mesh, in_specs=in_specs, out_specs=out_specs, check_vma=False
    )
```

```python
import jax
import jax.numpy as jnp
from jax import lax
from jax.experimental import pallas as pl
from jax.experimental.pallas import tpu as pltpu
from jax.sharding import PartitionSpec as P

TG = 8
TR = 16
TC = 16
CH = 128
STEPS = 4
PIX = TR * TC
EXT = (TR + 2) * TC
SLOTS = TR + 4
MESH = pl.DeviceIdType.MESH
BF = jnp.bfloat16
F32 = jnp.float32

NEAR = TR + 2
FAR_DELTAS = ((-1, -1), (-1, 1), (1, -1), (1, 1), (-1, 0), (1, 0))
NEAR_DELTAS = ((0, -1), (0, 1))
DELTAS = FAR_DELTAS + NEAR_DELTAS


def kernel(
    sections,
    tiles,
    frames_ref,
    weights_ref,
    bias_ref,
    cot_ref,
    hidden_ref,
    grads_ref,
    xin,
    hin,
    dzin,
    din,
    hcol,
    dzcol,
    hcor,
    fcor,
    zcor,
    xcin,
    hcin,
    zcin,
    dsend,
    fcol,
    wf,
    wb,
    pick,
    pick_far,
    edge,
    win_f,
    win_b,
    far_f,
    far_b,
    z_ref,
    du_ref,
    dc_ref,
    gates,
    cells,
    cot_t,
    x_sem,
    h_sem,
    dz_sem,
    xt_sem,
    d_sem,
    fs_sem,
    xs_sem,
    hs_sem,
    xts_sem,
    dzs_sem,
    ds_sem,
    w_sem,
):
    sec = lax.axis_index("section")
    tile = lax.axis_index("tile")
    grid_rows = tiles // TG
    row = lax.div(tile, TG)
    col = lax.rem(tile, TG)
    first = sec == 0
    last = sec == sections - 1

    def at(delta_row, delta_col):
        there_row = lax.rem(row + (delta_row + grid_rows), grid_rows)
        there_col = lax.rem(col + (delta_col + TG), TG)
        return there_row * TG + there_col

    copies = []
    for a in range(3):
        for b in range(3):
            copies.append(
                pltpu.make_async_copy(
                    weights_ref.at[3 * a + b], wf.at[a, :, pl.ds(2 * CH * b, 2 * CH)], w_sem.at[0, 3 * a + b]
                )
            )
            copies.append(
                pltpu.make_async_copy(
                    weights_ref.at[3 * a + 2 - b], wb.at[a, pl.ds(4 * CH * b, 4 * CH), :], w_sem.at[1, 3 * a + b]
                )
            )
    for copy in copies:
        copy.start()

    hin[0] = jnp.zeros(hin.shape[1:], BF)
    for buf in (xin, hin, dzin):
        buf[:, TR:SLOTS] = jnp.zeros((buf.shape[0], SLOTS - TR, TC, buf.shape[3]), BF)
    for buf in (xcin, hcin, zcin):
        buf[...] = jnp.zeros(buf.shape, F32)

    barrier = pltpu.get_barrier_semaphore()
    for delta in DELTAS:
        pl.semaphore_signal(barrier, inc=1, device_id={"section": sec, "tile": at(*delta)}, device_id_type=MESH)

    @pl.when(sec > 0)
    def _():
        for delta in DELTAS:
            pl.semaphore_signal(
                barrier, inc=1, device_id={"section": sec - 1, "tile": at(*delta)}, device_id_type=MESH
            )
        pl.semaphore_signal(barrier, inc=1, device_id={"section": sec - 1, "tile": tile}, device_id_type=MESH)

    @pl.when(sec < sections - 1)
    def _():
        pl.semaphore_signal(barrier, inc=1, device_id={"section": sec + 1, "tile": tile}, device_id_type=MESH)

    def exists(delta_row, delta_col):
        seen = jnp.bool_(True)
        if delta_row:
            seen = row > 0 if delta_row < 0 else row < grid_rows - 1
        if delta_col:
            seen_col = col > 0 if delta_col < 0 else col < TG - 1
            seen = seen & seen_col if delta_row else seen_col
        return seen

    out_at = lax.broadcasted_iota(jnp.int32, (PIX, NEAR * TC), 0)
    src_at = lax.broadcasted_iota(jnp.int32, (PIX, NEAR * TC), 1)
    r_at = lax.shift_right_logical(out_at, 4)
    q_at = lax.bitwise_and(out_at, TC - 1)
    for side in range(2):
        on_rim = q_at == (0 if side == 0 else TC - 1)
        source = jnp.where(on_rim, (TR + side) * TC + r_at, out_at + (2 * side - 1))
        pick[side] = jnp.where(src_at == source, 1.0, 0.0).astype(BF)
    out_at = lax.broadcasted_iota(jnp.int32, (2 * TC, 2 * TC), 0)
    src_at = lax.broadcasted_iota(jnp.int32, (2 * TC, 2 * TC), 1)
    for side in range(2):
        pick_far[side] = jnp.where(src_at == out_at + (2 * side - 1), 1.0, 0.0).astype(BF)
    edge_out = lax.broadcasted_iota(jnp.int32, (2 * TR, PIX), 0)
    edge_src = lax.broadcasted_iota(jnp.int32, (2 * TR, PIX), 1)
    edge_want = jnp.where(edge_out < TR, edge_out * TC, (edge_out - TR) * TC + TC - 1)
    edge[...] = jnp.where(edge_src == edge_want, 1.0, 0.0).astype(BF)

    def columns(field):
        return jnp.dot(edge[...], field, preferred_element_type=F32).astype(BF)

    def rims(deltas, tile_buf, col_buf, cor_buf, dst, dst_cor, section, send_sem, recv_sem):
        for delta_row, delta_col in deltas:
            k = DELTAS.index((delta_row, delta_col))
            if k < 4:
                piece, there = cor_buf.at[3 - k], dst_cor.at[k]
            elif delta_row:
                piece = tile_buf.at[TR - 1 if delta_row < 0 else 0]
                there = dst.at[18 if delta_row < 0 else 19]
            else:
                piece = col_buf.at[1 if delta_col < 0 else 0]
                there = dst.at[16 if delta_col < 0 else 17]

            @pl.when(exists(-delta_row, -delta_col))
            def _():
                pltpu.make_async_remote_copy(
                    src_ref=piece,
                    dst_ref=there,
                    send_sem=send_sem.at[k],
                    recv_sem=recv_sem.at[k],
                    device_id={"section": section, "tile": at(-delta_row, -delta_col)},
                    device_id_type=MESH,
                ).start()

    def settle_rims(deltas, buf, cor, sems, sign=1):
        for delta_row, delta_col in deltas:
            k = DELTAS.index((delta_row, delta_col))

            @pl.when(exists(sign * delta_row, sign * delta_col))
            def _():
                wait_for(cor.at[k] if k < 4 else buf.at[TR], sems.at[k])

    def set_corners(cor, top, low):
        cor[0] = top[0:1].astype(F32)
        cor[1] = top[TC - 1 : TC].astype(F32)
        cor[2] = low[0:1].astype(F32)
        cor[3] = low[TC - 1 : TC].astype(F32)

    def wait_for(buf, sem):
        pltpu.make_async_copy(buf, buf, sem).wait()

    def turn_cotangent():
        def turn(t, carry):
            cot_t[t] = cot_ref[t].astype(F32).T
            return carry

        lax.fori_loop(0, STEPS, turn, 0)

    for win in (win_f, win_b):
        rim = jnp.zeros((TC, win.shape[1]), BF)
        win[0:TC, :] = rim
        win[TC + PIX : EXT, :] = rim

    @pl.when(first)
    def _():
        def place(t, carry):
            field = frames_ref[t].astype(F32).T.astype(BF)
            xin[t, 0:TR] = field.reshape(TR, TC, CH)
            fcol[t] = columns(field).reshape(2, TR, CH)
            set_corners(fcor.at[t], field[:TC].astype(F32), field[PIX - TC :].astype(F32))
            return carry

        lax.fori_loop(0, STEPS, place, 0)

    @pl.when(sec > 0)
    def _():
        turn_cotangent()

    pl.semaphore_wait(
        barrier,
        8 + jnp.where(last, 0, 9) + jnp.where(first, 0, 1),
    )

    @pl.when(first)
    def _():
        def share(t, carry):
            rims(DELTAS, xin.at[t], fcol.at[t], fcor.at[t], xin.at[t], xcin.at[t], sec, fs_sem.at[t], x_sem.at[t])
            return carry

        lax.fori_loop(0, STEPS, share, 0)

    for copy in copies[0::2]:
        copy.wait()

    def spread(buf, t, width, win, base, stride):
        whole = buf[t, 0:NEAR].reshape(NEAR * TC, width)
        for side in range(2):
            moved = jnp.dot(pick[side], whole, preferred_element_type=F32).astype(BF)
            win[TC : TC + PIX, pl.ds(2 * side * stride + base, width)] = moved
        win[TC : TC + PIX, pl.ds(stride + base, width)] = whole[:PIX]

    def spread_far(buf, cor, t, width, win, base, stride):
        whole = buf[t, NEAR:SLOTS].reshape(2 * TC, width)
        q_at = lax.broadcasted_iota(jnp.int32, (TC, width), 0)
        for side in range(2):
            moved = jnp.dot(pick_far[side], whole, preferred_element_type=F32)
            rim = q_at == (0 if side == 0 else TC - 1)
            for low in range(2):
                cell = jnp.broadcast_to(cor[t, 2 * low + side], (TC, width))
                part = jnp.where(rim, cell, moved[low * TC : (low + 1) * TC])
                win[low * TC : (low + 1) * TC, pl.ds(2 * side * stride + base, width)] = part.astype(BF)
        win[:, pl.ds(stride + base, width)] = whole

    cells[0] = jnp.zeros((PIX, CH), F32)

    def send_rows(buf, buf_t, dst, dst_t, start, count, section, send_sem, recv_sem):
        pltpu.make_async_remote_copy(
            src_ref=buf.at[buf_t, pl.ds(start, count)],
            dst_ref=dst.at[dst_t, pl.ds(start, count)],
            send_sem=send_sem,
            recv_sem=recv_sem,
            device_id={"section": section, "tile": tile},
            device_id_type=MESH,
        ).start()

    def advance(t, low, high):
        z = z_ref[low:high, :]
        in_gate = jax.nn.sigmoid(z[:, :CH])
        forget = jax.nn.sigmoid(z[:, CH : 2 * CH])
        cand = jnp.tanh(z[:, 2 * CH : 3 * CH])
        out_gate = jax.nn.sigmoid(z[:, 3 * CH :])
        cell = forget * cells[t, low:high, :] + in_gate * cand
        hidden = (out_gate * jnp.tanh(cell)).astype(BF)
        hin[t + 1, low // TC : high // TC] = hidden.reshape((high - low) // TC, TC, CH)
        gates[t, low:high, 0:CH] = in_gate
        gates[t, low:high, CH : 2 * CH] = forget
        gates[t, low:high, 2 * CH : 3 * CH] = cand
        gates[t, low:high, 3 * CH :] = out_gate
        cells[t + 1, low:high, :] = cell
        return hidden.astype(F32)

    def forward(t, carry):
        @pl.when(t > 0)
        def _():
            settle_rims(NEAR_DELTAS, hin.at[t], hcin.at[t], h_sem.at[t])

        spread(hin, t, CH, win_f, CH, 2 * CH)

        @pl.when(sec > 0)
        def _():
            wait_for(xin.at[t, pl.ds(1, TR - 2)], xt_sem.at[t, 0])
            wait_for(xin.at[t, pl.ds(0, 2)], xt_sem.at[t, 1])

        settle_rims(NEAR_DELTAS, xin.at[t], xcin.at[t], x_sem.at[t])
        spread(xin, t, CH, win_f, 0, 2 * CH)
        z = bias_ref[...]
        for a in range(3):
            z = z + lax.dot_general(
                win_f[a * TC : a * TC + PIX, :],
                wf[a],
                (((1,), (1,)), ((), ())),
                preferred_element_type=F32,
            )
        z_ref[...] = z
        advance(t, TC, PIX - TC)

        @pl.when(sec < sections - 1)
        def _():
            send_rows(hin, t + 1, xin, t, 1, TR - 2, sec + 1, xts_sem.at[t, 0], xt_sem.at[t, 0])

        @pl.when(t > 0)
        def _():
            settle_rims(FAR_DELTAS, hin.at[t], hcin.at[t], h_sem.at[t])

        settle_rims(FAR_DELTAS, xin.at[t], xcin.at[t], x_sem.at[t])
        spread_far(hin, hcin, t, CH, far_f, CH, 2 * CH)
        spread_far(xin, xcin, t, CH, far_f, 0, 2 * CH)
        for a, start in ((0, 0), (2, PIX - TC)):
            far = far_f[0:TC, :] if a == 0 else far_f[TC : 2 * TC, :]
            z_ref[start : start + TC, :] += lax.dot_general(
                far, wf[a], (((1,), (1,)), ((), ())), preferred_element_type=F32
            )
        top = advance(t, 0, TC)
        low = advance(t, PIX - TC, PIX)
        set_corners(hcor.at[t], top, low)

        def share(deltas):
            @pl.when(sec < sections - 1)
            def _():
                rims(
                    deltas, hin.at[t + 1], hcol.at[t], hcor.at[t], xin.at[t], xcin.at[t], sec + 1, xs_sem.at[t], x_sem.at[t]
                )

            @pl.when(t < STEPS - 1)
            def _():
                rims(
                    deltas,
                    hin.at[t + 1],
                    hcol.at[t],
                    hcor.at[t],
                    hin.at[t + 1],
                    hcin.at[t + 1],
                    sec,
                    hs_sem.at[t],
                    h_sem.at[t + 1],
                )

        share(FAR_DELTAS)

        @pl.when(sec < sections - 1)
        def _():
            for edge_row in (0, TR - 1):
                send_rows(hin, t + 1, xin, t, edge_row, 1, sec + 1, xts_sem.at[t, 1], xt_sem.at[t, 1])

        field = hin[t + 1, 0:TR].reshape(PIX, CH)
        hcol[t] = columns(field).reshape(2, TR, CH)
        share(NEAR_DELTAS)
        hidden_ref[t] = field.astype(F32).T.astype(BF)
        return carry

    lax.fori_loop(0, STEPS, forward, 0)

    @pl.when(first)
    def _():
        turn_cotangent()

    for copy in copies[1::2]:
        copy.wait()

    def slope(t, low, high):
        in_gate = gates[t, low:high, 0:CH]
        forget = gates[t, low:high, CH : 2 * CH]
        cand = gates[t, low:high, 2 * CH : 3 * CH]
        out_gate = gates[t, low:high, 3 * CH :]
        tanh_cell = jnp.tanh(cells[t + 1, low:high, :])
        rows = (high - low) // TC
        from_above = din[t, low // TC : high // TC].reshape(high - low, CH).astype(F32)
        d_hidden = cot_t[t, low:high, :] + from_above + du_ref[low:high, CH:]
        d_total = dc_ref[low:high, :] + d_hidden * out_gate * (1.0 - tanh_cell * tanh_cell)
        parts = [
            d_total * cand * in_gate * (1.0 - in_gate),
            d_total * cells[t, low:high, :] * forget * (1.0 - forget),
            d_total * in_gate * (1.0 - cand * cand),
            d_hidden * tanh_cell * out_gate * (1.0 - out_gate),
        ]
        dz = jnp.concatenate([part.astype(BF) for part in parts], 1)
        dc_ref[low:high, :] = d_total * forget
        dzin[t, low // TC : high // TC] = dz.reshape(rows, TC, 4 * CH)
        return dz.astype(F32)

    def backward(back, carry):
        t = STEPS - 1 - back

        @pl.when(sec < sections - 1)
        def _():
            wait_for(din.at[t, pl.ds(1, TR - 2)], d_sem.at[t, 0])

        slope(t, TC, PIX - TC)

        @pl.when(sec < sections - 1)
        def _():
            wait_for(din.at[t, pl.ds(0, 2)], d_sem.at[t, 1])

        top = slope(t, 0, TC)
        low = slope(t, PIX - TC, PIX)
        set_corners(zcor.at[t], top, low)

        def share(deltas):
            rims(
                deltas, dzin.at[t], dzcol.at[t], zcor.at[t], dzin.at[t], zcin.at[t], sec, dzs_sem.at[t], dz_sem.at[t]
            )

        share(FAR_DELTAS)
        dzcol[t] = columns(dzin[t, 0:TR].reshape(PIX, 4 * CH)).reshape(2, TR, 4 * CH)
        share(NEAR_DELTAS)
        settle_rims(NEAR_DELTAS, dzin.at[t], zcin.at[t], dz_sem.at[t])
        spread(dzin, t, 4 * CH, win_b, 0, 4 * CH)
        du = None
        for a in range(3):
            term = jnp.dot(
                win_b[(2 - a) * TC : (2 - a) * TC + PIX, :], wb[a], preferred_element_type=F32
            )
            du = term if du is None else du + term
        du_ref[...] = du
        dsend[t] = du[:, :CH].astype(BF).reshape(TR, TC, CH)
        above = (dsend, t, din, t)

        @pl.when(sec > 0)
        def _():
            send_rows(*above, 1, TR - 2, sec - 1, ds_sem.at[t, 0], d_sem.at[t, 0])

        settle_rims(FAR_DELTAS, dzin.at[t], zcin.at[t], dz_sem.at[t])
        spread_far(dzin, zcin, t, 4 * CH, far_b, 0, 4 * CH)
        for a, start in ((2, 0), (0, PIX - TC)):
            far = far_b[0:TC, :] if a == 2 else far_b[TC : 2 * TC, :]
            rim = du_ref[start : start + TC, :] + jnp.dot(far, wb[a], preferred_element_type=F32)
            du_ref[start : start + TC, :] = rim
            dsend[t, start // TC] = rim[:, :CH].astype(BF)

        @pl.when(sec > 0)
        def _():
            for edge_row in (0, TR - 1):
                send_rows(*above, edge_row, 1, sec - 1, ds_sem.at[t, 1], d_sem.at[t, 1])

        grads_ref[t] = du_ref[:, :CH].T.astype(BF)
        return carry

    @pl.when(last)
    def _():
        din[...] = jnp.zeros(din.shape, BF)

    du_ref[...] = jnp.zeros(du_ref.shape, F32)
    dc_ref[...] = jnp.zeros(dc_ref.shape, F32)
    lax.fori_loop(0, STEPS, backward, 0)

    def settle(t, carry):
        @pl.when(first)
        def _():
            settle_rims(DELTAS, xin.at[t], xcin.at[t], fs_sem.at[t], -1)

        @pl.when(sec < sections - 1)
        def _():
            settle_rims(DELTAS, xin.at[t], xcin.at[t], xs_sem.at[t], -1)
            wait_for(xin.at[t, pl.ds(1, TR - 2)], xts_sem.at[t, 0])
            wait_for(xin.at[t, pl.ds(0, 2)], xts_sem.at[t, 1])

        @pl.when(t < STEPS - 1)
        def _():
            settle_rims(DELTAS, hin.at[t], hcin.at[t], hs_sem.at[t], -1)

        settle_rims(DELTAS, dzin.at[t], zcin.at[t], dzs_sem.at[t], -1)

        @pl.when(sec > 0)
        def _():
            wait_for(dsend.at[t, pl.ds(1, TR - 2)], ds_sem.at[t, 0])
            wait_for(dsend.at[t, pl.ds(0, 2)], ds_sem.at[t, 1])

        return carry

    lax.fori_loop(0, STEPS, settle, 0)


def make_step(sections, tiles):
    def body(*refs):
        kernel(sections, tiles, *refs)

    return pl.pallas_call(
        body,
        out_shape=[jax.ShapeDtypeStruct((STEPS, CH, PIX), BF)] * 2,
        in_specs=[
            pl.BlockSpec(memory_space=pltpu.VMEM),
            pl.BlockSpec(memory_space=pl.ANY),
            pl.BlockSpec(memory_space=pltpu.VMEM),
            pl.BlockSpec(memory_space=pltpu.VMEM),
        ],
        out_specs=[pl.BlockSpec(memory_space=pltpu.VMEM)] * 2,
        scratch_shapes=[
            pltpu.VMEM((STEPS, SLOTS, TC, CH), BF),
            pltpu.VMEM((STEPS + 1, SLOTS, TC, CH), BF),
            pltpu.VMEM((STEPS, SLOTS, TC, 4 * CH), BF),
            pltpu.VMEM((STEPS, TR, TC, CH), BF),
            pltpu.VMEM((STEPS, 2, TR, CH), BF),
            pltpu.VMEM((STEPS, 2, TR, 4 * CH), BF),
            pltpu.VMEM((STEPS, 4, 1, CH), F32),
            pltpu.VMEM((STEPS, 4, 1, CH), F32),
            pltpu.VMEM((STEPS, 4, 1, 4 * CH), F32),
            pltpu.VMEM((STEPS, 4, 1, CH), F32),
            pltpu.VMEM((STEPS, 4, 1, CH), F32),
            pltpu.VMEM((STEPS, 4, 1, 4 * CH), F32),
            pltpu.VMEM((STEPS, TR, TC, CH), BF),
            pltpu.VMEM((STEPS, 2, TR, CH), BF),
            pltpu.VMEM((3, 4 * CH, 6 * CH), BF),
            pltpu.VMEM((3, 12 * CH, 2 * CH), BF),
            pltpu.VMEM((2, PIX, NEAR * TC), BF),
            pltpu.VMEM((2, 2 * TC, 2 * TC), BF),
            pltpu.VMEM((2 * TR, PIX), BF),
            pltpu.VMEM((EXT, 6 * CH), BF),
            pltpu.VMEM((EXT, 12 * CH), BF),
            pltpu.VMEM((2 * TC, 6 * CH), BF),
            pltpu.VMEM((2 * TC, 12 * CH), BF),
            pltpu.VMEM((PIX, 4 * CH), F32),
            pltpu.VMEM((PIX, 2 * CH), F32),
            pltpu.VMEM((PIX, CH), F32),
            pltpu.VMEM((STEPS, PIX, 4 * CH), F32),
            pltpu.VMEM((STEPS + 1, PIX, CH), F32),
            pltpu.VMEM((STEPS, PIX, CH), F32),
            pltpu.SemaphoreType.DMA((STEPS, 8)),
            pltpu.SemaphoreType.DMA((STEPS, 8)),
            pltpu.SemaphoreType.DMA((STEPS, 8)),
            pltpu.SemaphoreType.DMA((STEPS, 2)),
            pltpu.SemaphoreType.DMA((STEPS, 2)),
            pltpu.SemaphoreType.DMA((STEPS, 8)),
            pltpu.SemaphoreType.DMA((STEPS, 8)),
            pltpu.SemaphoreType.DMA((STEPS, 8)),
            pltpu.SemaphoreType.DMA((STEPS, 2)),
            pltpu.SemaphoreType.DMA((STEPS, 8)),
            pltpu.SemaphoreType.DMA((STEPS, 2)),
            pltpu.SemaphoreType.DMA((2, 9)),
        ],
        compiler_params=pltpu.CompilerParams(
            collective_id=0, has_side_effects=True, vmem_limit_bytes=56 * 1024 * 1024
        ),
        name="conv_lstm",
    )


def solution(mesh):
    step = make_step(mesh.shape["section"], mesh.shape["tile"])

    def per_device(frames, weights, gate_bias, cotangent):
        hidden, grads = step(
            frames.reshape(STEPS, CH, PIX), weights[0], gate_bias, cotangent.reshape(STEPS, CH, PIX)
        )
        shape = (1, STEPS, CH, 1, PIX)
        return hidden.reshape(shape), grads.reshape(shape)

    in_specs = (
        P(None, None, "tile", None),
        P("section", None, None, None),
        P("section", None),
        P("section", None, None, "tile", None),
    )
    out_specs = (P("section", None, None, "tile", None), P("section", None, None, "tile", None))
    return jax.shard_map(
        per_device, mesh=mesh, in_specs=in_specs, out_specs=out_specs, check_vma=False
    )
```

```python
import jax
import jax.numpy as jnp
from jax import lax
from jax.experimental import pallas as pl
from jax.experimental.pallas import tpu as pltpu
from jax.sharding import PartitionSpec as P

TG = 8
TR = 16
TC = 16
CH = 128
STEPS = 4
PIX = TR * TC
EXT = (TR + 2) * TC
SLOTS = TR + 4
MESH = pl.DeviceIdType.MESH
BF = jnp.bfloat16
F32 = jnp.float32

NEAR = TR + 2
FAR_DELTAS = ((-1, -1), (-1, 1), (1, -1), (1, 1), (-1, 0), (1, 0))
NEAR_DELTAS = ((0, -1), (0, 1))
DELTAS = FAR_DELTAS + NEAR_DELTAS


def kernel(
    sections,
    tiles,
    frames_ref,
    weights_ref,
    bias_ref,
    cot_ref,
    hidden_ref,
    grads_ref,
    xin,
    hin,
    dzin,
    din,
    hcol,
    dzcol,
    hcor,
    fcor,
    zcor,
    xcin,
    hcin,
    zcin,
    frames_in,
    cot_in,
    stage,
    land,
    dsend,
    fcol,
    wf,
    wb,
    pick,
    pick_far,
    edge,
    win_f,
    win_b,
    far_f,
    far_b,
    z_ref,
    du_ref,
    dc_ref,
    gates,
    cells,
    cot_t,
    x_sem,
    h_sem,
    dz_sem,
    xt_sem,
    d_sem,
    fs_sem,
    xs_sem,
    hs_sem,
    xts_sem,
    dzs_sem,
    ds_sem,
    w_sem,
    fin_sem,
    cin_sem,
    out_sem,
):
    sec = lax.axis_index("section")
    tile = lax.axis_index("tile")
    grid_rows = tiles // TG
    half = grid_rows // 2

    def mirror(grid_row):
        return jnp.where(grid_row >= half, half + grid_rows - 1 - grid_row, grid_row)

    stored_row = lax.div(tile, TG)
    swapped = stored_row >= half
    kept = stored_row < half
    row = mirror(stored_row)
    col = lax.rem(tile, TG)
    first = sec == 0
    last = sec == sections - 1

    def at(delta_row, delta_col):
        there_row = lax.rem(row + (delta_row + grid_rows), grid_rows)
        there_col = lax.rem(col + (delta_col + TG), TG)
        return mirror(there_row) * TG + there_col

    partner = {"section": sec, "tile": row * TG + col}

    copies = []
    for a in range(3):
        for b in range(3):
            copies.append(
                pltpu.make_async_copy(
                    weights_ref.at[3 * a + b], wf.at[a, :, pl.ds(2 * CH * b, 2 * CH)], w_sem.at[0, 3 * a + b]
                )
            )
            copies.append(
                pltpu.make_async_copy(
                    weights_ref.at[3 * a + 2 - b], wb.at[a, pl.ds(4 * CH * b, 4 * CH), :], w_sem.at[1, 3 * a + b]
                )
            )
    for copy in copies:
        copy.start()

    hin[0] = jnp.zeros(hin.shape[1:], BF)
    for buf in (xin, hin, dzin):
        buf[:, TR:SLOTS] = jnp.zeros((buf.shape[0], SLOTS - TR, TC, buf.shape[3]), BF)
    for buf in (xcin, hcin, zcin):
        buf[...] = jnp.zeros(buf.shape, F32)

    barrier = pltpu.get_barrier_semaphore()
    for delta in DELTAS:
        pl.semaphore_signal(barrier, inc=1, device_id={"section": sec, "tile": at(*delta)}, device_id_type=MESH)

    @pl.when(sec > 0)
    def _():
        for delta in DELTAS:
            pl.semaphore_signal(
                barrier, inc=1, device_id={"section": sec - 1, "tile": at(*delta)}, device_id_type=MESH
            )
        pl.semaphore_signal(barrier, inc=1, device_id={"section": sec - 1, "tile": tile}, device_id_type=MESH)

    @pl.when(sec < sections - 1)
    def _():
        pl.semaphore_signal(barrier, inc=1, device_id={"section": sec + 1, "tile": tile}, device_id_type=MESH)

    def exists(delta_row, delta_col):
        seen = jnp.bool_(True)
        if delta_row:
            seen = row > 0 if delta_row < 0 else row < grid_rows - 1
        if delta_col:
            seen_col = col > 0 if delta_col < 0 else col < TG - 1
            seen = seen & seen_col if delta_row else seen_col
        return seen

    @pl.when(swapped)
    def _():
        pl.semaphore_signal(barrier, inc=1, device_id=partner, device_id_type=MESH)

    out_at = lax.broadcasted_iota(jnp.int32, (PIX, NEAR * TC), 0)
    src_at = lax.broadcasted_iota(jnp.int32, (PIX, NEAR * TC), 1)
    r_at = lax.shift_right_logical(out_at, 4)
    q_at = lax.bitwise_and(out_at, TC - 1)
    for side in range(2):
        on_rim = q_at == (0 if side == 0 else TC - 1)
        source = jnp.where(on_rim, (TR + side) * TC + r_at, out_at + (2 * side - 1))
        pick[side] = jnp.where(src_at == source, 1.0, 0.0).astype(BF)
    out_at = lax.broadcasted_iota(jnp.int32, (2 * TC, 2 * TC), 0)
    src_at = lax.broadcasted_iota(jnp.int32, (2 * TC, 2 * TC), 1)
    for side in range(2):
        pick_far[side] = jnp.where(src_at == out_at + (2 * side - 1), 1.0, 0.0).astype(BF)
    edge_out = lax.broadcasted_iota(jnp.int32, (2 * TR, PIX), 0)
    edge_src = lax.broadcasted_iota(jnp.int32, (2 * TR, PIX), 1)
    edge_want = jnp.where(edge_out < TR, edge_out * TC, (edge_out - TR) * TC + TC - 1)
    edge[...] = jnp.where(edge_src == edge_want, 1.0, 0.0).astype(BF)

    def columns(field):
        return jnp.dot(edge[...], field, preferred_element_type=F32).astype(BF)

    def rims(deltas, tile_buf, col_buf, cor_buf, dst, dst_cor, section, send_sem, recv_sem):
        for delta_row, delta_col in deltas:
            k = DELTAS.index((delta_row, delta_col))
            if k < 4:
                piece, there = cor_buf.at[3 - k], dst_cor.at[k]
            elif delta_row:
                piece = tile_buf.at[TR - 1 if delta_row < 0 else 0]
                there = dst.at[18 if delta_row < 0 else 19]
            else:
                piece = col_buf.at[1 if delta_col < 0 else 0]
                there = dst.at[16 if delta_col < 0 else 17]

            @pl.when(exists(-delta_row, -delta_col))
            def _():
                pltpu.make_async_remote_copy(
                    src_ref=piece,
                    dst_ref=there,
                    send_sem=send_sem.at[k],
                    recv_sem=recv_sem.at[k],
                    device_id={"section": section, "tile": at(-delta_row, -delta_col)},
                    device_id_type=MESH,
                ).start()

    def settle_rims(deltas, buf, cor, sems, sign=1):
        for delta_row, delta_col in deltas:
            k = DELTAS.index((delta_row, delta_col))

            @pl.when(exists(sign * delta_row, sign * delta_col))
            def _():
                wait_for(cor.at[k] if k < 4 else buf.at[TR], sems.at[k])

    def set_corners(cor, top, low):
        cor[0] = top[0:1].astype(F32)
        cor[1] = top[TC - 1 : TC].astype(F32)
        cor[2] = low[0:1].astype(F32)
        cor[3] = low[TC - 1 : TC].astype(F32)

    def wait_for(buf, sem):
        pltpu.make_async_copy(buf, buf, sem).wait()

    def turn_cotangent(source):
        def turn(t, carry):
            cot_t[t] = source[t].astype(F32).T
            return carry

        lax.fori_loop(0, STEPS, turn, 0)

    def to_partner(src, dst, send_sem, recv_sem):
        return pltpu.make_async_remote_copy(
            src_ref=src,
            dst_ref=dst,
            send_sem=send_sem,
            recv_sem=recv_sem,
            device_id=partner,
            device_id_type=MESH,
        )

    def emit(which, out_ref, t, field):
        value = field.reshape(PIX, CH).astype(F32).T.astype(BF)

        @pl.when(swapped)
        def _():
            stage[which, t] = value
            to_partner(stage.at[which, t], land.at[which, t], out_sem.at[0, which, t], out_sem.at[1, which, t]).start()

        @pl.when(kept)
        def _():
            out_ref[t] = value

    for win in (win_f, win_b):
        rim = jnp.zeros((TC, win.shape[1]), BF)
        win[0:TC, :] = rim
        win[TC + PIX : EXT, :] = rim

    def place(source, t):
        field = source[t].astype(F32).T.astype(BF)
        xin[t, 0:TR] = field.reshape(TR, TC, CH)
        fcol[t] = columns(field).reshape(2, TR, CH)
        set_corners(fcor.at[t], field[:TC].astype(F32), field[PIX - TC :].astype(F32))

    @pl.when(first & kept)
    def _():
        def place_own(t, carry):
            place(frames_ref, t)
            return carry

        lax.fori_loop(0, STEPS, place_own, 0)

    early = (sec > 0) & kept

    @pl.when(early)
    def _():
        turn_cotangent(cot_ref)

    pl.semaphore_wait(
        barrier,
        8 + jnp.where(last, 0, 9) + jnp.where(first, 0, 1) + jnp.where(swapped, 1, 0),
    )

    @pl.when(first & swapped)
    def _():
        for t in range(STEPS):
            to_partner(frames_ref.at[t], frames_in.at[t], fin_sem.at[0, t], fin_sem.at[1, t]).start()

    @pl.when(swapped)
    def _():
        to_partner(cot_ref, cot_in, cin_sem.at[0], cin_sem.at[1]).start()

    @pl.when(first)
    def _():
        def share(t, carry):
            @pl.when(swapped)
            def _():
                wait_for(frames_in.at[t], fin_sem.at[1, t])
                place(frames_in, t)

            rims(DELTAS, xin.at[t], fcol.at[t], fcor.at[t], xin.at[t], xcin.at[t], sec, fs_sem.at[t], x_sem.at[t])
            return carry

        lax.fori_loop(0, STEPS, share, 0)

    for copy in copies[0::2]:
        copy.wait()

    def spread(buf, t, width, win, base, stride):
        whole = buf[t, 0:NEAR].reshape(NEAR * TC, width)
        for side in range(2):
            moved = jnp.dot(pick[side], whole, preferred_element_type=F32).astype(BF)
            win[TC : TC + PIX, pl.ds(2 * side * stride + base, width)] = moved
        win[TC : TC + PIX, pl.ds(stride + base, width)] = whole[:PIX]

    def spread_far(buf, cor, t, width, win, base, stride):
        whole = buf[t, NEAR:SLOTS].reshape(2 * TC, width)
        q_at = lax.broadcasted_iota(jnp.int32, (TC, width), 0)
        for side in range(2):
            moved = jnp.dot(pick_far[side], whole, preferred_element_type=F32)
            rim = q_at == (0 if side == 0 else TC - 1)
            for low in range(2):
                cell = jnp.broadcast_to(cor[t, 2 * low + side], (TC, width))
                part = jnp.where(rim, cell, moved[low * TC : (low + 1) * TC])
                win[low * TC : (low + 1) * TC, pl.ds(2 * side * stride + base, width)] = part.astype(BF)
        win[:, pl.ds(stride + base, width)] = whole

    cells[0] = jnp.zeros((PIX, CH), F32)

    def send_rows(buf, buf_t, dst, dst_t, start, count, section, send_sem, recv_sem):
        pltpu.make_async_remote_copy(
            src_ref=buf.at[buf_t, pl.ds(start, count)],
            dst_ref=dst.at[dst_t, pl.ds(start, count)],
            send_sem=send_sem,
            recv_sem=recv_sem,
            device_id={"section": section, "tile": tile},
            device_id_type=MESH,
        ).start()

    def advance(t, low, high):
        z = z_ref[low:high, :]
        in_gate = jax.nn.sigmoid(z[:, :CH])
        forget = jax.nn.sigmoid(z[:, CH : 2 * CH])
        cand = jnp.tanh(z[:, 2 * CH : 3 * CH])
        out_gate = jax.nn.sigmoid(z[:, 3 * CH :])
        cell = forget * cells[t, low:high, :] + in_gate * cand
        hidden = (out_gate * jnp.tanh(cell)).astype(BF)
        hin[t + 1, low // TC : high // TC] = hidden.reshape((high - low) // TC, TC, CH)
        gates[t, low:high, 0:CH] = in_gate
        gates[t, low:high, CH : 2 * CH] = forget
        gates[t, low:high, 2 * CH : 3 * CH] = cand
        gates[t, low:high, 3 * CH :] = out_gate
        cells[t + 1, low:high, :] = cell
        return hidden.astype(F32)

    def forward(t, carry):
        @pl.when(t > 0)
        def _():
            settle_rims(NEAR_DELTAS, hin.at[t], hcin.at[t], h_sem.at[t])

        spread(hin, t, CH, win_f, CH, 2 * CH)

        @pl.when(sec > 0)
        def _():
            wait_for(xin.at[t, pl.ds(1, TR - 2)], xt_sem.at[t, 0])
            wait_for(xin.at[t, pl.ds(0, 2)], xt_sem.at[t, 1])

        settle_rims(NEAR_DELTAS, xin.at[t], xcin.at[t], x_sem.at[t])
        spread(xin, t, CH, win_f, 0, 2 * CH)
        z = bias_ref[...]
        for a in range(3):
            z = z + lax.dot_general(
                win_f[a * TC : a * TC + PIX, :],
                wf[a],
                (((1,), (1,)), ((), ())),
                preferred_element_type=F32,
            )
        z_ref[...] = z
        advance(t, TC, PIX - TC)

        @pl.when(sec < sections - 1)
        def _():
            send_rows(hin, t + 1, xin, t, 1, TR - 2, sec + 1, xts_sem.at[t, 0], xt_sem.at[t, 0])

        @pl.when(t > 0)
        def _():
            settle_rims(FAR_DELTAS, hin.at[t], hcin.at[t], h_sem.at[t])

        settle_rims(FAR_DELTAS, xin.at[t], xcin.at[t], x_sem.at[t])
        spread_far(hin, hcin, t, CH, far_f, CH, 2 * CH)
        spread_far(xin, xcin, t, CH, far_f, 0, 2 * CH)
        for a, start in ((0, 0), (2, PIX - TC)):
            far = far_f[0:TC, :] if a == 0 else far_f[TC : 2 * TC, :]
            z_ref[start : start + TC, :] += lax.dot_general(
                far, wf[a], (((1,), (1,)), ((), ())), preferred_element_type=F32
            )
        top = advance(t, 0, TC)
        low = advance(t, PIX - TC, PIX)
        set_corners(hcor.at[t], top, low)

        def share(deltas):
            @pl.when(sec < sections - 1)
            def _():
                rims(
                    deltas, hin.at[t + 1], hcol.at[t], hcor.at[t], xin.at[t], xcin.at[t], sec + 1, xs_sem.at[t], x_sem.at[t]
                )

            @pl.when(t < STEPS - 1)
            def _():
                rims(
                    deltas,
                    hin.at[t + 1],
                    hcol.at[t],
                    hcor.at[t],
                    hin.at[t + 1],
                    hcin.at[t + 1],
                    sec,
                    hs_sem.at[t],
                    h_sem.at[t + 1],
                )

        share(FAR_DELTAS)

        @pl.when(sec < sections - 1)
        def _():
            for edge_row in (0, TR - 1):
                send_rows(hin, t + 1, xin, t, edge_row, 1, sec + 1, xts_sem.at[t, 1], xt_sem.at[t, 1])

        field = hin[t + 1, 0:TR].reshape(PIX, CH)
        hcol[t] = columns(field).reshape(2, TR, CH)
        share(NEAR_DELTAS)
        return carry

    lax.fori_loop(0, STEPS, forward, 0)

    @pl.when(swapped)
    def _():
        wait_for(cot_in, cin_sem.at[1])
        turn_cotangent(cot_in)

    @pl.when(first & kept)
    def _():
        turn_cotangent(cot_ref)

    for copy in copies[1::2]:
        copy.wait()

    def slope(t, low, high):
        in_gate = gates[t, low:high, 0:CH]
        forget = gates[t, low:high, CH : 2 * CH]
        cand = gates[t, low:high, 2 * CH : 3 * CH]
        out_gate = gates[t, low:high, 3 * CH :]
        tanh_cell = jnp.tanh(cells[t + 1, low:high, :])
        rows = (high - low) // TC
        from_above = din[t, low // TC : high // TC].reshape(high - low, CH).astype(F32)
        d_hidden = cot_t[t, low:high, :] + from_above + du_ref[low:high, CH:]
        d_total = dc_ref[low:high, :] + d_hidden * out_gate * (1.0 - tanh_cell * tanh_cell)
        parts = [
            d_total * cand * in_gate * (1.0 - in_gate),
            d_total * cells[t, low:high, :] * forget * (1.0 - forget),
            d_total * in_gate * (1.0 - cand * cand),
            d_hidden * tanh_cell * out_gate * (1.0 - out_gate),
        ]
        dz = jnp.concatenate([part.astype(BF) for part in parts], 1)
        dc_ref[low:high, :] = d_total * forget
        dzin[t, low // TC : high // TC] = dz.reshape(rows, TC, 4 * CH)
        return dz.astype(F32)

    def backward(back, carry):
        t = STEPS - 1 - back

        @pl.when(sec < sections - 1)
        def _():
            wait_for(din.at[t, pl.ds(1, TR - 2)], d_sem.at[t, 0])

        slope(t, TC, PIX - TC)

        @pl.when(sec < sections - 1)
        def _():
            wait_for(din.at[t, pl.ds(0, 2)], d_sem.at[t, 1])

        top = slope(t, 0, TC)
        low = slope(t, PIX - TC, PIX)
        set_corners(zcor.at[t], top, low)

        def share(deltas):
            rims(
                deltas, dzin.at[t], dzcol.at[t], zcor.at[t], dzin.at[t], zcin.at[t], sec, dzs_sem.at[t], dz_sem.at[t]
            )

        share(FAR_DELTAS)
        dzcol[t] = columns(dzin[t, 0:TR].reshape(PIX, 4 * CH)).reshape(2, TR, 4 * CH)
        share(NEAR_DELTAS)
        emit(0, hidden_ref, t, hin[t + 1, 0:TR])

        @pl.when(back > 0)
        def _():
            emit(1, grads_ref, t + 1, dsend[t + 1])

        settle_rims(NEAR_DELTAS, dzin.at[t], zcin.at[t], dz_sem.at[t])
        spread(dzin, t, 4 * CH, win_b, 0, 4 * CH)
        du = None
        for a in range(3):
            term = jnp.dot(
                win_b[(2 - a) * TC : (2 - a) * TC + PIX, :], wb[a], preferred_element_type=F32
            )
            du = term if du is None else du + term
        du_ref[...] = du
        dsend[t] = du[:, :CH].astype(BF).reshape(TR, TC, CH)
        above = (dsend, t, din, t)

        @pl.when(sec > 0)
        def _():
            send_rows(*above, 1, TR - 2, sec - 1, ds_sem.at[t, 0], d_sem.at[t, 0])

        settle_rims(FAR_DELTAS, dzin.at[t], zcin.at[t], dz_sem.at[t])
        spread_far(dzin, zcin, t, 4 * CH, far_b, 0, 4 * CH)
        for a, start in ((2, 0), (0, PIX - TC)):
            far = far_b[0:TC, :] if a == 2 else far_b[TC : 2 * TC, :]
            rim = du_ref[start : start + TC, :] + jnp.dot(far, wb[a], preferred_element_type=F32)
            du_ref[start : start + TC, :] = rim
            dsend[t, start // TC] = rim[:, :CH].astype(BF)

        @pl.when(sec > 0)
        def _():
            for edge_row in (0, TR - 1):
                send_rows(*above, edge_row, 1, sec - 1, ds_sem.at[t, 1], d_sem.at[t, 1])

        return carry

    @pl.when(last)
    def _():
        din[...] = jnp.zeros(din.shape, BF)

    du_ref[...] = jnp.zeros(du_ref.shape, F32)
    dc_ref[...] = jnp.zeros(dc_ref.shape, F32)
    lax.fori_loop(0, STEPS, backward, 0)
    emit(1, grads_ref, 0, dsend[0])

    def settle(t, carry):
        @pl.when(first)
        def _():
            settle_rims(DELTAS, xin.at[t], xcin.at[t], fs_sem.at[t], -1)

        @pl.when(sec < sections - 1)
        def _():
            settle_rims(DELTAS, xin.at[t], xcin.at[t], xs_sem.at[t], -1)
            wait_for(xin.at[t, pl.ds(1, TR - 2)], xts_sem.at[t, 0])
            wait_for(xin.at[t, pl.ds(0, 2)], xts_sem.at[t, 1])

        @pl.when(t < STEPS - 1)
        def _():
            settle_rims(DELTAS, hin.at[t], hcin.at[t], hs_sem.at[t], -1)

        settle_rims(DELTAS, dzin.at[t], zcin.at[t], dzs_sem.at[t], -1)

        @pl.when(sec > 0)
        def _():
            wait_for(dsend.at[t, pl.ds(1, TR - 2)], ds_sem.at[t, 0])
            wait_for(dsend.at[t, pl.ds(0, 2)], ds_sem.at[t, 1])

        return carry

    lax.fori_loop(0, STEPS, settle, 0)

    @pl.when(first & swapped)
    def _():
        for t in range(STEPS):
            wait_for(frames_in.at[t], fin_sem.at[0, t])

    @pl.when(swapped)
    def _():
        wait_for(cot_in, cin_sem.at[0])

        def fetch(t, carry):
            for which, out_ref in enumerate((hidden_ref, grads_ref)):
                wait_for(stage.at[which, t], out_sem.at[0, which, t])
                wait_for(land.at[which, t], out_sem.at[1, which, t])
                out_ref[t] = land[which, t]
            return carry

        lax.fori_loop(0, STEPS, fetch, 0)


def make_step(sections, tiles):
    def body(*refs):
        kernel(sections, tiles, *refs)

    return pl.pallas_call(
        body,
        out_shape=[jax.ShapeDtypeStruct((STEPS, CH, PIX), BF)] * 2,
        in_specs=[
            pl.BlockSpec(memory_space=pltpu.VMEM),
            pl.BlockSpec(memory_space=pl.ANY),
            pl.BlockSpec(memory_space=pltpu.VMEM),
            pl.BlockSpec(memory_space=pltpu.VMEM),
        ],
        out_specs=[pl.BlockSpec(memory_space=pltpu.VMEM)] * 2,
        scratch_shapes=[
            pltpu.VMEM((STEPS, SLOTS, TC, CH), BF),
            pltpu.VMEM((STEPS + 1, SLOTS, TC, CH), BF),
            pltpu.VMEM((STEPS, SLOTS, TC, 4 * CH), BF),
            pltpu.VMEM((STEPS, TR, TC, CH), BF),
            pltpu.VMEM((STEPS, 2, TR, CH), BF),
            pltpu.VMEM((STEPS, 2, TR, 4 * CH), BF),
            pltpu.VMEM((STEPS, 4, 1, CH), F32),
            pltpu.VMEM((STEPS, 4, 1, CH), F32),
            pltpu.VMEM((STEPS, 4, 1, 4 * CH), F32),
            pltpu.VMEM((STEPS, 4, 1, CH), F32),
            pltpu.VMEM((STEPS, 4, 1, CH), F32),
            pltpu.VMEM((STEPS, 4, 1, 4 * CH), F32),
            pltpu.VMEM((STEPS, CH, PIX), BF),
            pltpu.VMEM((STEPS, CH, PIX), BF),
            pltpu.VMEM((2, STEPS, CH, PIX), BF),
            pltpu.VMEM((2, STEPS, CH, PIX), BF),
            pltpu.VMEM((STEPS, TR, TC, CH), BF),
            pltpu.VMEM((STEPS, 2, TR, CH), BF),
            pltpu.VMEM((3, 4 * CH, 6 * CH), BF),
            pltpu.VMEM((3, 12 * CH, 2 * CH), BF),
            pltpu.VMEM((2, PIX, NEAR * TC), BF),
            pltpu.VMEM((2, 2 * TC, 2 * TC), BF),
            pltpu.VMEM((2 * TR, PIX), BF),
            pltpu.VMEM((EXT, 6 * CH), BF),
            pltpu.VMEM((EXT, 12 * CH), BF),
            pltpu.VMEM((2 * TC, 6 * CH), BF),
            pltpu.VMEM((2 * TC, 12 * CH), BF),
            pltpu.VMEM((PIX, 4 * CH), F32),
            pltpu.VMEM((PIX, 2 * CH), F32),
            pltpu.VMEM((PIX, CH), F32),
            pltpu.VMEM((STEPS, PIX, 4 * CH), F32),
            pltpu.VMEM((STEPS + 1, PIX, CH), F32),
            pltpu.VMEM((STEPS, PIX, CH), F32),
            pltpu.SemaphoreType.DMA((STEPS, 8)),
            pltpu.SemaphoreType.DMA((STEPS, 8)),
            pltpu.SemaphoreType.DMA((STEPS, 8)),
            pltpu.SemaphoreType.DMA((STEPS, 2)),
            pltpu.SemaphoreType.DMA((STEPS, 2)),
            pltpu.SemaphoreType.DMA((STEPS, 8)),
            pltpu.SemaphoreType.DMA((STEPS, 8)),
            pltpu.SemaphoreType.DMA((STEPS, 8)),
            pltpu.SemaphoreType.DMA((STEPS, 2)),
            pltpu.SemaphoreType.DMA((STEPS, 8)),
            pltpu.SemaphoreType.DMA((STEPS, 2)),
            pltpu.SemaphoreType.DMA((2, 9)),
            pltpu.SemaphoreType.DMA((2, STEPS)),
            pltpu.SemaphoreType.DMA((2,)),
            pltpu.SemaphoreType.DMA((2, 2, STEPS)),
        ],
        compiler_params=pltpu.CompilerParams(
            collective_id=0, has_side_effects=True, vmem_limit_bytes=56 * 1024 * 1024
        ),
        name="conv_lstm",
    )


def solution(mesh):
    step = make_step(mesh.shape["section"], mesh.shape["tile"])

    def per_device(frames, weights, gate_bias, cotangent):
        hidden, grads = step(
            frames.reshape(STEPS, CH, PIX), weights[0], gate_bias, cotangent.reshape(STEPS, CH, PIX)
        )
        shape = (1, STEPS, CH, 1, PIX)
        return hidden.reshape(shape), grads.reshape(shape)

    in_specs = (
        P(None, None, "tile", None),
        P("section", None, None, None),
        P("section", None),
        P("section", None, None, "tile", None),
    )
    out_specs = (P("section", None, None, "tile", None), P("section", None, None, "tile", None))
    return jax.shard_map(
        per_device, mesh=mesh, in_specs=in_specs, out_specs=out_specs, check_vma=False
    )
```

```python
import jax
import jax.numpy as jnp
from jax import lax
from jax.experimental import pallas as pl
from jax.experimental.pallas import tpu as pltpu
from jax.sharding import PartitionSpec as P

TG = 8
TR = 16
TC = 16
CH = 128
STEPS = 4
PIX = TR * TC
EXT = (TR + 2) * TC
SLOTS = TR + 4
MESH = pl.DeviceIdType.MESH
BF = jnp.bfloat16
F32 = jnp.float32

NEAR = TR + 2
FAR_DELTAS = ((-1, -1), (-1, 1), (1, -1), (1, 1), (-1, 0), (1, 0))
NEAR_DELTAS = ((0, -1), (0, 1))
ABOVE = ((-1, -1), (-1, 1), (-1, 0))
BELOW = ((1, -1), (1, 1), (1, 0))
DELTAS = FAR_DELTAS + NEAR_DELTAS


def kernel(
    sections,
    tiles,
    frames_ref,
    weights_ref,
    bias_ref,
    cot_ref,
    hidden_ref,
    grads_ref,
    xin,
    hin,
    dzin,
    din,
    hcol,
    dzcol,
    hcor,
    fcor,
    zcor,
    xcin,
    hcin,
    zcin,
    frames_in,
    cot_in,
    stage,
    land,
    dsend,
    fcol,
    wf,
    wb,
    pick,
    pick_far,
    edge,
    win_f,
    win_b,
    far_f,
    far_b,
    z_ref,
    du_ref,
    dc_ref,
    gates,
    cells,
    cot_t,
    x_sem,
    h_sem,
    dz_sem,
    xt_sem,
    d_sem,
    fs_sem,
    xs_sem,
    hs_sem,
    xts_sem,
    dzs_sem,
    ds_sem,
    w_sem,
    fin_sem,
    cin_sem,
    out_sem,
):
    sec = lax.axis_index("section")
    tile = lax.axis_index("tile")
    grid_rows = tiles // TG
    half = grid_rows // 2

    def mirror(grid_row):
        return jnp.where(grid_row >= half, half + grid_rows - 1 - grid_row, grid_row)

    stored_row = lax.div(tile, TG)
    swapped = stored_row >= half
    kept = stored_row < half
    row = mirror(stored_row)
    col = lax.rem(tile, TG)
    first = sec == 0
    last = sec == sections - 1

    def at(delta_row, delta_col):
        there_row = lax.rem(row + (delta_row + grid_rows), grid_rows)
        there_col = lax.rem(col + (delta_col + TG), TG)
        return mirror(there_row) * TG + there_col

    partner = {"section": sec, "tile": row * TG + col}

    copies = []
    for a in range(3):
        for b in range(3):
            copies.append(
                pltpu.make_async_copy(
                    weights_ref.at[3 * a + b], wf.at[a, :, pl.ds(2 * CH * b, 2 * CH)], w_sem.at[0, 3 * a + b]
                )
            )
            copies.append(
                pltpu.make_async_copy(
                    weights_ref.at[3 * a + 2 - b], wb.at[a, pl.ds(4 * CH * b, 4 * CH), :], w_sem.at[1, 3 * a + b]
                )
            )
    for copy in copies:
        copy.start()

    hin[0] = jnp.zeros(hin.shape[1:], BF)
    for buf in (xin, hin, dzin):
        buf[:, TR:SLOTS] = jnp.zeros((buf.shape[0], SLOTS - TR, TC, buf.shape[3]), BF)
    for buf in (xcin, hcin, zcin):
        buf[...] = jnp.zeros(buf.shape, F32)

    barrier = pltpu.get_barrier_semaphore()
    for delta in DELTAS:
        pl.semaphore_signal(barrier, inc=1, device_id={"section": sec, "tile": at(*delta)}, device_id_type=MESH)

    @pl.when(sec > 0)
    def _():
        for delta in DELTAS:
            pl.semaphore_signal(
                barrier, inc=1, device_id={"section": sec - 1, "tile": at(*delta)}, device_id_type=MESH
            )
        pl.semaphore_signal(barrier, inc=1, device_id={"section": sec - 1, "tile": tile}, device_id_type=MESH)

    @pl.when(sec < sections - 1)
    def _():
        pl.semaphore_signal(barrier, inc=1, device_id={"section": sec + 1, "tile": tile}, device_id_type=MESH)

    def exists(delta_row, delta_col):
        seen = jnp.bool_(True)
        if delta_row:
            seen = row > 0 if delta_row < 0 else row < grid_rows - 1
        if delta_col:
            seen_col = col > 0 if delta_col < 0 else col < TG - 1
            seen = seen & seen_col if delta_row else seen_col
        return seen

    @pl.when(swapped)
    def _():
        pl.semaphore_signal(barrier, inc=1, device_id=partner, device_id_type=MESH)

    out_at = lax.broadcasted_iota(jnp.int32, (PIX, NEAR * TC), 0)
    src_at = lax.broadcasted_iota(jnp.int32, (PIX, NEAR * TC), 1)
    r_at = lax.shift_right_logical(out_at, 4)
    q_at = lax.bitwise_and(out_at, TC - 1)
    for side in range(2):
        on_rim = q_at == (0 if side == 0 else TC - 1)
        source = jnp.where(on_rim, (TR + side) * TC + r_at, out_at + (2 * side - 1))
        pick[side] = jnp.where(src_at == source, 1.0, 0.0).astype(BF)
    out_at = lax.broadcasted_iota(jnp.int32, (TC, TC), 0)
    src_at = lax.broadcasted_iota(jnp.int32, (TC, TC), 1)
    for side in range(2):
        pick_far[side] = jnp.where(src_at == out_at + (2 * side - 1), 1.0, 0.0).astype(BF)
    edge_out = lax.broadcasted_iota(jnp.int32, (2 * TR, PIX), 0)
    edge_src = lax.broadcasted_iota(jnp.int32, (2 * TR, PIX), 1)
    edge_want = jnp.where(edge_out < TR, edge_out * TC, (edge_out - TR) * TC + TC - 1)
    edge[...] = jnp.where(edge_src == edge_want, 1.0, 0.0).astype(BF)

    def columns(field):
        return jnp.dot(edge[...], field, preferred_element_type=F32).astype(BF)

    def rims(deltas, tile_buf, col_buf, cor_buf, dst, dst_cor, section, send_sem, recv_sem):
        for delta_row, delta_col in deltas:
            k = DELTAS.index((delta_row, delta_col))
            if k < 4:
                piece, there = cor_buf.at[3 - k], dst_cor.at[k]
            elif delta_row:
                piece = tile_buf.at[TR - 1 if delta_row < 0 else 0]
                there = dst.at[18 if delta_row < 0 else 19]
            else:
                piece = col_buf.at[1 if delta_col < 0 else 0]
                there = dst.at[16 if delta_col < 0 else 17]

            @pl.when(exists(-delta_row, -delta_col))
            def _():
                pltpu.make_async_remote_copy(
                    src_ref=piece,
                    dst_ref=there,
                    send_sem=send_sem.at[k],
                    recv_sem=recv_sem.at[k],
                    device_id={"section": section, "tile": at(-delta_row, -delta_col)},
                    device_id_type=MESH,
                ).start()

    def settle_rims(deltas, buf, cor, sems, sign=1):
        for delta_row, delta_col in deltas:
            k = DELTAS.index((delta_row, delta_col))

            @pl.when(exists(sign * delta_row, sign * delta_col))
            def _():
                wait_for(cor.at[k] if k < 4 else buf.at[TR], sems.at[k])

    def set_corners(cor, side, rim):
        cor[2 * side] = rim[0:1]
        cor[2 * side + 1] = rim[TC - 1 : TC]

    def both_sides(work):
        @pl.when(kept)
        def _():
            work(0)
            work(1)

        @pl.when(swapped)
        def _():
            work(1)
            work(0)

    def wait_for(buf, sem):
        pltpu.make_async_copy(buf, buf, sem).wait()

    def turn_cotangent(source):
        def turn(t, carry):
            cot_t[t] = source[t].astype(F32).T
            return carry

        lax.fori_loop(0, STEPS, turn, 0)

    def to_partner(src, dst, send_sem, recv_sem):
        return pltpu.make_async_remote_copy(
            src_ref=src,
            dst_ref=dst,
            send_sem=send_sem,
            recv_sem=recv_sem,
            device_id=partner,
            device_id_type=MESH,
        )

    def emit(which, out_ref, t, field):
        value = field.reshape(PIX, CH).astype(F32).T.astype(BF)

        @pl.when(swapped)
        def _():
            stage[which, t] = value
            to_partner(stage.at[which, t], land.at[which, t], out_sem.at[0, which, t], out_sem.at[1, which, t]).start()

        @pl.when(kept)
        def _():
            out_ref[t] = value

    for win in (win_f, win_b):
        rim = jnp.zeros((TC, win.shape[1]), BF)
        win[0:TC, :] = rim
        win[TC + PIX : EXT, :] = rim

    def place(source, t):
        field = source[t].astype(F32).T.astype(BF)
        xin[t, 0:TR] = field.reshape(TR, TC, CH)
        fcol[t] = columns(field).reshape(2, TR, CH)
        set_corners(fcor.at[t], 0, field[:TC].astype(F32))
        set_corners(fcor.at[t], 1, field[PIX - TC :].astype(F32))

    @pl.when(first & kept)
    def _():
        def place_own(t, carry):
            place(frames_ref, t)
            return carry

        lax.fori_loop(0, STEPS, place_own, 0)

    early = (sec > 0) & kept

    @pl.when(early)
    def _():
        turn_cotangent(cot_ref)

    pl.semaphore_wait(
        barrier,
        8 + jnp.where(last, 0, 9) + jnp.where(first, 0, 1) + jnp.where(swapped, 1, 0),
    )

    @pl.when(first & swapped)
    def _():
        for t in range(STEPS):
            to_partner(frames_ref.at[t], frames_in.at[t], fin_sem.at[0, t], fin_sem.at[1, t]).start()

    @pl.when(swapped)
    def _():
        to_partner(cot_ref, cot_in, cin_sem.at[0], cin_sem.at[1]).start()

    @pl.when(first)
    def _():
        def share(t, carry):
            @pl.when(swapped)
            def _():
                wait_for(frames_in.at[t], fin_sem.at[1, t])
                place(frames_in, t)

            rims(DELTAS, xin.at[t], fcol.at[t], fcor.at[t], xin.at[t], xcin.at[t], sec, fs_sem.at[t], x_sem.at[t])
            return carry

        lax.fori_loop(0, STEPS, share, 0)

    for copy in copies[0::2]:
        copy.wait()

    def spread(buf, t, width, win, base, stride):
        whole = buf[t, 0:NEAR].reshape(NEAR * TC, width)
        for side in range(2):
            moved = jnp.dot(pick[side], whole, preferred_element_type=F32).astype(BF)
            win[TC : TC + PIX, pl.ds(2 * side * stride + base, width)] = moved
        win[TC : TC + PIX, pl.ds(stride + base, width)] = whole[:PIX]

    def spread_far(low, buf, cor, t, width, win, base, stride):
        whole = buf[t, NEAR + low]
        q_at = lax.broadcasted_iota(jnp.int32, (TC, width), 0)
        for side in range(2):
            moved = jnp.dot(pick_far[side], whole, preferred_element_type=F32)
            rim = q_at == (0 if side == 0 else TC - 1)
            cell = jnp.broadcast_to(cor[t, 2 * low + side], (TC, width))
            part = jnp.where(rim, cell, moved)
            win[low * TC : (low + 1) * TC, pl.ds(2 * side * stride + base, width)] = part.astype(BF)
        win[low * TC : (low + 1) * TC, pl.ds(stride + base, width)] = whole

    cells[0] = jnp.zeros((PIX, CH), F32)

    def send_rows(buf, buf_t, dst, dst_t, start, count, section, send_sem, recv_sem):
        pltpu.make_async_remote_copy(
            src_ref=buf.at[buf_t, pl.ds(start, count)],
            dst_ref=dst.at[dst_t, pl.ds(start, count)],
            send_sem=send_sem,
            recv_sem=recv_sem,
            device_id={"section": section, "tile": tile},
            device_id_type=MESH,
        ).start()

    def advance(t, low, high):
        z = z_ref[low:high, :]
        in_gate = jax.nn.sigmoid(z[:, :CH])
        forget = jax.nn.sigmoid(z[:, CH : 2 * CH])
        cand = jnp.tanh(z[:, 2 * CH : 3 * CH])
        out_gate = jax.nn.sigmoid(z[:, 3 * CH :])
        cell = forget * cells[t, low:high, :] + in_gate * cand
        hidden = (out_gate * jnp.tanh(cell)).astype(BF)
        hin[t + 1, low // TC : high // TC] = hidden.reshape((high - low) // TC, TC, CH)
        gates[t, low:high, 0:CH] = in_gate
        gates[t, low:high, CH : 2 * CH] = forget
        gates[t, low:high, 2 * CH : 3 * CH] = cand
        gates[t, low:high, 3 * CH :] = out_gate
        cells[t + 1, low:high, :] = cell
        return hidden.astype(F32)

    def forward(t, carry):
        @pl.when(t > 0)
        def _():
            settle_rims(NEAR_DELTAS, hin.at[t], hcin.at[t], h_sem.at[t])

        spread(hin, t, CH, win_f, CH, 2 * CH)

        @pl.when(sec > 0)
        def _():
            wait_for(xin.at[t, pl.ds(1, TR - 2)], xt_sem.at[t, 0])
            wait_for(xin.at[t, pl.ds(0, 1)], xt_sem.at[t, 1])
            wait_for(xin.at[t, pl.ds(0, 1)], xt_sem.at[t, 2])

        settle_rims(NEAR_DELTAS, xin.at[t], xcin.at[t], x_sem.at[t])
        spread(xin, t, CH, win_f, 0, 2 * CH)
        z = bias_ref[...]
        for a in range(3):
            z = z + lax.dot_general(
                win_f[a * TC : a * TC + PIX, :],
                wf[a],
                (((1,), (1,)), ((), ())),
                preferred_element_type=F32,
            )
        z_ref[...] = z
        advance(t, TC, PIX - TC)

        @pl.when(sec < sections - 1)
        def _():
            send_rows(hin, t + 1, xin, t, 1, TR - 2, sec + 1, xts_sem.at[t, 0], xt_sem.at[t, 0])

        def share(deltas):
            @pl.when(sec < sections - 1)
            def _():
                rims(
                    deltas, hin.at[t + 1], hcol.at[t], hcor.at[t], xin.at[t], xcin.at[t], sec + 1, xs_sem.at[t], x_sem.at[t]
                )

            @pl.when(t < STEPS - 1)
            def _():
                rims(
                    deltas,
                    hin.at[t + 1],
                    hcol.at[t],
                    hcor.at[t],
                    hin.at[t + 1],
                    hcin.at[t + 1],
                    sec,
                    hs_sem.at[t],
                    h_sem.at[t + 1],
                )

        def finish(side):
            deltas = BELOW if side else ABOVE
            start = side * (PIX - TC)

            @pl.when(t > 0)
            def _():
                settle_rims(deltas, hin.at[t], hcin.at[t], h_sem.at[t])

            settle_rims(deltas, xin.at[t], xcin.at[t], x_sem.at[t])
            spread_far(side, hin, hcin, t, CH, far_f, CH, 2 * CH)
            spread_far(side, xin, xcin, t, CH, far_f, 0, 2 * CH)
            z_ref[start : start + TC, :] += lax.dot_general(
                far_f[side * TC : (side + 1) * TC, :],
                wf[2 * side],
                (((1,), (1,)), ((), ())),
                preferred_element_type=F32,
            )
            set_corners(hcor.at[t], side, advance(t, start, start + TC))
            share(ABOVE if side else BELOW)

            @pl.when(sec < sections - 1)
            def _():
                send_rows(hin, t + 1, xin, t, side * (TR - 1), 1, sec + 1, xts_sem.at[t, 1 + side], xt_sem.at[t, 1 + side])

        both_sides(finish)
        field = hin[t + 1, 0:TR].reshape(PIX, CH)
        hcol[t] = columns(field).reshape(2, TR, CH)
        share(NEAR_DELTAS)
        return carry

    lax.fori_loop(0, STEPS, forward, 0)

    @pl.when(swapped)
    def _():
        wait_for(cot_in, cin_sem.at[1])
        turn_cotangent(cot_in)

    @pl.when(first & kept)
    def _():
        turn_cotangent(cot_ref)

    for copy in copies[1::2]:
        copy.wait()

    def slope(t, low, high):
        in_gate = gates[t, low:high, 0:CH]
        forget = gates[t, low:high, CH : 2 * CH]
        cand = gates[t, low:high, 2 * CH : 3 * CH]
        out_gate = gates[t, low:high, 3 * CH :]
        tanh_cell = jnp.tanh(cells[t + 1, low:high, :])
        rows = (high - low) // TC
        from_above = din[t, low // TC : high // TC].reshape(high - low, CH).astype(F32)
        d_hidden = cot_t[t, low:high, :] + from_above + du_ref[low:high, CH:]
        d_total = dc_ref[low:high, :] + d_hidden * out_gate * (1.0 - tanh_cell * tanh_cell)
        parts = [
            d_total * cand * in_gate * (1.0 - in_gate),
            d_total * cells[t, low:high, :] * forget * (1.0 - forget),
            d_total * in_gate * (1.0 - cand * cand),
            d_hidden * tanh_cell * out_gate * (1.0 - out_gate),
        ]
        dz = jnp.concatenate([part.astype(BF) for part in parts], 1)
        dc_ref[low:high, :] = d_total * forget
        dzin[t, low // TC : high // TC] = dz.reshape(rows, TC, 4 * CH)
        return dz.astype(F32)

    def backward(back, carry):
        t = STEPS - 1 - back

        @pl.when(sec < sections - 1)
        def _():
            wait_for(din.at[t, pl.ds(1, TR - 2)], d_sem.at[t, 0])

        slope(t, TC, PIX - TC)

        def share(deltas):
            rims(
                deltas, dzin.at[t], dzcol.at[t], zcor.at[t], dzin.at[t], zcin.at[t], sec, dzs_sem.at[t], dz_sem.at[t]
            )

        def begin(side):
            start = side * (PIX - TC)

            @pl.when(sec < sections - 1)
            def _():
                wait_for(din.at[t, pl.ds(0, 1)], d_sem.at[t, 1 + side])

            set_corners(zcor.at[t], side, slope(t, start, start + TC))
            share(ABOVE if side else BELOW)

        both_sides(begin)
        dzcol[t] = columns(dzin[t, 0:TR].reshape(PIX, 4 * CH)).reshape(2, TR, 4 * CH)
        share(NEAR_DELTAS)
        emit(0, hidden_ref, t, hin[t + 1, 0:TR])

        @pl.when(back > 0)
        def _():
            emit(1, grads_ref, t + 1, dsend[t + 1])

        settle_rims(NEAR_DELTAS, dzin.at[t], zcin.at[t], dz_sem.at[t])
        spread(dzin, t, 4 * CH, win_b, 0, 4 * CH)
        du = None
        for a in range(3):
            term = jnp.dot(
                win_b[(2 - a) * TC : (2 - a) * TC + PIX, :], wb[a], preferred_element_type=F32
            )
            du = term if du is None else du + term
        du_ref[...] = du
        dsend[t] = du[:, :CH].astype(BF).reshape(TR, TC, CH)
        above = (dsend, t, din, t)

        @pl.when(sec > 0)
        def _():
            send_rows(*above, 1, TR - 2, sec - 1, ds_sem.at[t, 0], d_sem.at[t, 0])

        def finish(side):
            start = side * (PIX - TC)
            settle_rims(BELOW if side else ABOVE, dzin.at[t], zcin.at[t], dz_sem.at[t])
            spread_far(side, dzin, zcin, t, 4 * CH, far_b, 0, 4 * CH)
            rim = du_ref[start : start + TC, :] + jnp.dot(
                far_b[side * TC : (side + 1) * TC, :], wb[2 - 2 * side], preferred_element_type=F32
            )
            du_ref[start : start + TC, :] = rim
            dsend[t, side * (TR - 1)] = rim[:, :CH].astype(BF)

            @pl.when(sec > 0)
            def _():
                send_rows(*above, side * (TR - 1), 1, sec - 1, ds_sem.at[t, 1 + side], d_sem.at[t, 1 + side])

        both_sides(finish)
        return carry

    @pl.when(last)
    def _():
        din[...] = jnp.zeros(din.shape, BF)

    du_ref[...] = jnp.zeros(du_ref.shape, F32)
    dc_ref[...] = jnp.zeros(dc_ref.shape, F32)
    lax.fori_loop(0, STEPS, backward, 0)
    emit(1, grads_ref, 0, dsend[0])

    def settle(t, carry):
        @pl.when(first)
        def _():
            settle_rims(DELTAS, xin.at[t], xcin.at[t], fs_sem.at[t], -1)

        @pl.when(sec < sections - 1)
        def _():
            settle_rims(DELTAS, xin.at[t], xcin.at[t], xs_sem.at[t], -1)
            wait_for(xin.at[t, pl.ds(1, TR - 2)], xts_sem.at[t, 0])
            wait_for(xin.at[t, pl.ds(0, 1)], xts_sem.at[t, 1])
            wait_for(xin.at[t, pl.ds(0, 1)], xts_sem.at[t, 2])

        @pl.when(t < STEPS - 1)
        def _():
            settle_rims(DELTAS, hin.at[t], hcin.at[t], hs_sem.at[t], -1)

        settle_rims(DELTAS, dzin.at[t], zcin.at[t], dzs_sem.at[t], -1)

        @pl.when(sec > 0)
        def _():
            wait_for(dsend.at[t, pl.ds(1, TR - 2)], ds_sem.at[t, 0])
            wait_for(dsend.at[t, pl.ds(0, 1)], ds_sem.at[t, 1])
            wait_for(dsend.at[t, pl.ds(0, 1)], ds_sem.at[t, 2])

        return carry

    lax.fori_loop(0, STEPS, settle, 0)

    @pl.when(first & swapped)
    def _():
        for t in range(STEPS):
            wait_for(frames_in.at[t], fin_sem.at[0, t])

    @pl.when(swapped)
    def _():
        wait_for(cot_in, cin_sem.at[0])

        def fetch(t, carry):
            for which, out_ref in enumerate((hidden_ref, grads_ref)):
                wait_for(stage.at[which, t], out_sem.at[0, which, t])
                wait_for(land.at[which, t], out_sem.at[1, which, t])
                out_ref[t] = land[which, t]
            return carry

        lax.fori_loop(0, STEPS, fetch, 0)


def make_step(sections, tiles):
    def body(*refs):
        kernel(sections, tiles, *refs)

    return pl.pallas_call(
        body,
        out_shape=[jax.ShapeDtypeStruct((STEPS, CH, PIX), BF)] * 2,
        in_specs=[
            pl.BlockSpec(memory_space=pltpu.VMEM),
            pl.BlockSpec(memory_space=pl.ANY),
            pl.BlockSpec(memory_space=pltpu.VMEM),
            pl.BlockSpec(memory_space=pltpu.VMEM),
        ],
        out_specs=[pl.BlockSpec(memory_space=pltpu.VMEM)] * 2,
        scratch_shapes=[
            pltpu.VMEM((STEPS, SLOTS, TC, CH), BF),
            pltpu.VMEM((STEPS + 1, SLOTS, TC, CH), BF),
            pltpu.VMEM((STEPS, SLOTS, TC, 4 * CH), BF),
            pltpu.VMEM((STEPS, TR, TC, CH), BF),
            pltpu.VMEM((STEPS, 2, TR, CH), BF),
            pltpu.VMEM((STEPS, 2, TR, 4 * CH), BF),
            pltpu.VMEM((STEPS, 4, 1, CH), F32),
            pltpu.VMEM((STEPS, 4, 1, CH), F32),
            pltpu.VMEM((STEPS, 4, 1, 4 * CH), F32),
            pltpu.VMEM((STEPS, 4, 1, CH), F32),
            pltpu.VMEM((STEPS, 4, 1, CH), F32),
            pltpu.VMEM((STEPS, 4, 1, 4 * CH), F32),
            pltpu.VMEM((STEPS, CH, PIX), BF),
            pltpu.VMEM((STEPS, CH, PIX), BF),
            pltpu.VMEM((2, STEPS, CH, PIX), BF),
            pltpu.VMEM((2, STEPS, CH, PIX), BF),
            pltpu.VMEM((STEPS, TR, TC, CH), BF),
            pltpu.VMEM((STEPS, 2, TR, CH), BF),
            pltpu.VMEM((3, 4 * CH, 6 * CH), BF),
            pltpu.VMEM((3, 12 * CH, 2 * CH), BF),
            pltpu.VMEM((2, PIX, NEAR * TC), BF),
            pltpu.VMEM((2, TC, TC), BF),
            pltpu.VMEM((2 * TR, PIX), BF),
            pltpu.VMEM((EXT, 6 * CH), BF),
            pltpu.VMEM((EXT, 12 * CH), BF),
            pltpu.VMEM((2 * TC, 6 * CH), BF),
            pltpu.VMEM((2 * TC, 12 * CH), BF),
            pltpu.VMEM((PIX, 4 * CH), F32),
            pltpu.VMEM((PIX, 2 * CH), F32),
            pltpu.VMEM((PIX, CH), F32),
            pltpu.VMEM((STEPS, PIX, 4 * CH), F32),
            pltpu.VMEM((STEPS + 1, PIX, CH), F32),
            pltpu.VMEM((STEPS, PIX, CH), F32),
            pltpu.SemaphoreType.DMA((STEPS, 8)),
            pltpu.SemaphoreType.DMA((STEPS, 8)),
            pltpu.SemaphoreType.DMA((STEPS, 8)),
            pltpu.SemaphoreType.DMA((STEPS, 3)),
            pltpu.SemaphoreType.DMA((STEPS, 3)),
            pltpu.SemaphoreType.DMA((STEPS, 8)),
            pltpu.SemaphoreType.DMA((STEPS, 8)),
            pltpu.SemaphoreType.DMA((STEPS, 8)),
            pltpu.SemaphoreType.DMA((STEPS, 3)),
            pltpu.SemaphoreType.DMA((STEPS, 8)),
            pltpu.SemaphoreType.DMA((STEPS, 3)),
            pltpu.SemaphoreType.DMA((2, 9)),
            pltpu.SemaphoreType.DMA((2, STEPS)),
            pltpu.SemaphoreType.DMA((2,)),
            pltpu.SemaphoreType.DMA((2, 2, STEPS)),
        ],
        compiler_params=pltpu.CompilerParams(
            collective_id=0, has_side_effects=True, vmem_limit_bytes=56 * 1024 * 1024
        ),
        name="conv_lstm",
    )


def solution(mesh):
    step = make_step(mesh.shape["section"], mesh.shape["tile"])

    def per_device(frames, weights, gate_bias, cotangent):
        hidden, grads = step(
            frames.reshape(STEPS, CH, PIX), weights[0], gate_bias, cotangent.reshape(STEPS, CH, PIX)
        )
        shape = (1, STEPS, CH, 1, PIX)
        return hidden.reshape(shape), grads.reshape(shape)

    in_specs = (
        P(None, None, "tile", None),
        P("section", None, None, None),
        P("section", None),
        P("section", None, None, "tile", None),
    )
    out_specs = (P("section", None, None, "tile", None), P("section", None, None, "tile", None))
    return jax.shard_map(
        per_device, mesh=mesh, in_specs=in_specs, out_specs=out_specs, check_vma=False
    )
```

```python
import jax
import jax.numpy as jnp
from jax import lax
from jax.experimental import pallas as pl
from jax.experimental.pallas import tpu as pltpu
from jax.sharding import PartitionSpec as P

TG = 8
TR = 16
TC = 16
CH = 128
STEPS = 4
PIX = TR * TC
EXT = (TR + 2) * TC
SLOTS = TR + 4
MESH = pl.DeviceIdType.MESH
BF = jnp.bfloat16
F32 = jnp.float32

NEAR = TR + 2
FAR_DELTAS = ((-1, -1), (-1, 1), (1, -1), (1, 1), (-1, 0), (1, 0))
NEAR_DELTAS = ((0, -1), (0, 1))
ABOVE = ((-1, -1), (-1, 1), (-1, 0))
BELOW = ((1, -1), (1, 1), (1, 0))
DELTAS = FAR_DELTAS + NEAR_DELTAS


def kernel(
    sections,
    tiles,
    frames_ref,
    weights_ref,
    bias_ref,
    cot_ref,
    hidden_ref,
    grads_ref,
    xin,
    hin,
    dzin,
    din,
    hcol,
    dzcol,
    hcor,
    fcor,
    zcor,
    xcin,
    hcin,
    zcin,
    frames_in,
    cot_in,
    stage,
    land,
    dsend,
    fcol,
    wf,
    wb,
    pick,
    pick_far,
    edge,
    win_f,
    win_b,
    far_f,
    far_b,
    z_ref,
    du_ref,
    dc_ref,
    gates,
    cells,
    cot_t,
    x_sem,
    h_sem,
    dz_sem,
    xt_sem,
    d_sem,
    fs_sem,
    xs_sem,
    hs_sem,
    xts_sem,
    dzs_sem,
    ds_sem,
    w_sem,
    fin_sem,
    cin_sem,
    out_sem,
):
    sec = lax.axis_index("section")
    tile = lax.axis_index("tile")
    grid_rows = tiles // TG
    half = grid_rows // 2

    def mirror(grid_row):
        return jnp.where(grid_row >= half, half + grid_rows - 1 - grid_row, grid_row)

    stored_row = lax.div(tile, TG)
    swapped = stored_row >= half
    kept = stored_row < half
    row = mirror(stored_row)
    col = lax.rem(tile, TG)
    first = sec == 0
    last = sec == sections - 1

    def at(delta_row, delta_col):
        there_row = lax.rem(row + (delta_row + grid_rows), grid_rows)
        there_col = lax.rem(col + (delta_col + TG), TG)
        return mirror(there_row) * TG + there_col

    partner = {"section": sec, "tile": row * TG + col}

    copies = []
    for a in range(3):
        for b in range(3):
            copies.append(
                pltpu.make_async_copy(
                    weights_ref.at[3 * a + b], wf.at[a, :, pl.ds(2 * CH * b, 2 * CH)], w_sem.at[0, 3 * a + b]
                )
            )
            copies.append(
                pltpu.make_async_copy(
                    weights_ref.at[3 * a + 2 - b], wb.at[a, pl.ds(4 * CH * b, 4 * CH), :], w_sem.at[1, 3 * a + b]
                )
            )
    for copy in copies:
        copy.start()

    hin[0] = jnp.zeros(hin.shape[1:], BF)
    for buf in (xin, hin, dzin):
        buf[:, TR:SLOTS] = jnp.zeros((buf.shape[0], SLOTS - TR, TC, buf.shape[3]), BF)
    for buf in (xcin, hcin, zcin):
        buf[...] = jnp.zeros(buf.shape, F32)

    barrier = pltpu.get_barrier_semaphore()
    for delta in DELTAS:
        pl.semaphore_signal(barrier, inc=1, device_id={"section": sec, "tile": at(*delta)}, device_id_type=MESH)

    @pl.when(sec > 0)
    def _():
        for delta in DELTAS:
            pl.semaphore_signal(
                barrier, inc=1, device_id={"section": sec - 1, "tile": at(*delta)}, device_id_type=MESH
            )
        pl.semaphore_signal(barrier, inc=1, device_id={"section": sec - 1, "tile": tile}, device_id_type=MESH)

    @pl.when(sec < sections - 1)
    def _():
        pl.semaphore_signal(barrier, inc=1, device_id={"section": sec + 1, "tile": tile}, device_id_type=MESH)

    def exists(delta_row, delta_col):
        seen = jnp.bool_(True)
        if delta_row:
            seen = row > 0 if delta_row < 0 else row < grid_rows - 1
        if delta_col:
            seen_col = col > 0 if delta_col < 0 else col < TG - 1
            seen = seen & seen_col if delta_row else seen_col
        return seen

    @pl.when(swapped)
    def _():
        pl.semaphore_signal(barrier, inc=1, device_id=partner, device_id_type=MESH)

    out_at = lax.broadcasted_iota(jnp.int32, (PIX, NEAR * TC), 0)
    src_at = lax.broadcasted_iota(jnp.int32, (PIX, NEAR * TC), 1)
    r_at = lax.shift_right_logical(out_at, 4)
    q_at = lax.bitwise_and(out_at, TC - 1)
    for side in range(2):
        on_rim = q_at == (0 if side == 0 else TC - 1)
        source = jnp.where(on_rim, (TR + side) * TC + r_at, out_at + (2 * side - 1))
        pick[side] = jnp.where(src_at == source, 1.0, 0.0).astype(BF)
    out_at = lax.broadcasted_iota(jnp.int32, (TC, TC), 0)
    src_at = lax.broadcasted_iota(jnp.int32, (TC, TC), 1)
    for side in range(2):
        pick_far[side] = jnp.where(src_at == out_at + (2 * side - 1), 1.0, 0.0).astype(BF)
    edge_out = lax.broadcasted_iota(jnp.int32, (2 * TR, PIX), 0)
    edge_src = lax.broadcasted_iota(jnp.int32, (2 * TR, PIX), 1)
    edge_want = jnp.where(edge_out < TR, edge_out * TC, (edge_out - TR) * TC + TC - 1)
    edge[...] = jnp.where(edge_src == edge_want, 1.0, 0.0).astype(BF)

    def columns(field):
        return jnp.dot(edge[...], field, preferred_element_type=F32).astype(BF)

    def rims(deltas, tile_buf, col_buf, cor_buf, dst, dst_cor, section, send_sem, recv_sem):
        for delta_row, delta_col in deltas:
            k = DELTAS.index((delta_row, delta_col))
            if k < 4:
                piece, there = cor_buf.at[3 - k], dst_cor.at[k]
            elif delta_row:
                piece = tile_buf.at[TR - 1 if delta_row < 0 else 0]
                there = dst.at[18 if delta_row < 0 else 19]
            else:
                piece = col_buf.at[1 if delta_col < 0 else 0]
                there = dst.at[16 if delta_col < 0 else 17]

            @pl.when(exists(-delta_row, -delta_col))
            def _():
                pltpu.make_async_remote_copy(
                    src_ref=piece,
                    dst_ref=there,
                    send_sem=send_sem.at[k],
                    recv_sem=recv_sem.at[k],
                    device_id={"section": section, "tile": at(-delta_row, -delta_col)},
                    device_id_type=MESH,
                ).start()

    def settle_rims(deltas, buf, cor, sems, sign=1):
        for delta_row, delta_col in deltas:
            k = DELTAS.index((delta_row, delta_col))

            @pl.when(exists(sign * delta_row, sign * delta_col))
            def _():
                wait_for(cor.at[k] if k < 4 else buf.at[TR], sems.at[k])

    def set_corners(cor, side, rim):
        cor[2 * side] = rim[0:1]
        cor[2 * side + 1] = rim[TC - 1 : TC]

    def both_sides(work):
        @pl.when(kept)
        def _():
            work(0)
            work(1)

        @pl.when(swapped)
        def _():
            work(1)
            work(0)

    def wait_for(buf, sem):
        pltpu.make_async_copy(buf, buf, sem).wait()

    def turn_cotangent(source):
        def turn(t, carry):
            cot_t[t] = source[t].astype(F32).T
            return carry

        lax.fori_loop(0, STEPS, turn, 0)

    def to_partner(src, dst, send_sem, recv_sem):
        return pltpu.make_async_remote_copy(
            src_ref=src,
            dst_ref=dst,
            send_sem=send_sem,
            recv_sem=recv_sem,
            device_id=partner,
            device_id_type=MESH,
        )

    def emit(which, out_ref, t, field):
        value = field.reshape(PIX, CH).astype(F32).T.astype(BF)

        @pl.when(swapped)
        def _():
            stage[which, t] = value
            to_partner(stage.at[which, t], land.at[which, t], out_sem.at[0, which, t], out_sem.at[1, which, t]).start()

        @pl.when(kept)
        def _():
            out_ref[t] = value

    for win in (win_f, win_b):
        rim = jnp.zeros((TC, win.shape[1]), BF)
        win[0:TC, :] = rim
        win[TC + PIX : EXT, :] = rim

    def place(source, t):
        field = source[t].astype(F32).T.astype(BF)
        xin[t, 0:TR] = field.reshape(TR, TC, CH)
        fcol[t] = columns(field).reshape(2, TR, CH)
        set_corners(fcor.at[t], 0, field[:TC].astype(F32))
        set_corners(fcor.at[t], 1, field[PIX - TC :].astype(F32))

    @pl.when(first & kept)
    def _():
        def place_own(t, carry):
            place(frames_ref, t)
            return carry

        lax.fori_loop(0, STEPS, place_own, 0)

    early = (sec > 0) & kept

    @pl.when(early)
    def _():
        turn_cotangent(cot_ref)

    pl.semaphore_wait(
        barrier,
        8 + jnp.where(last, 0, 9) + jnp.where(first, 0, 1) + jnp.where(swapped, 1, 0),
    )

    @pl.when(first & swapped)
    def _():
        for t in range(STEPS):
            to_partner(frames_ref.at[t], frames_in.at[t], fin_sem.at[0, t], fin_sem.at[1, t]).start()

    def enter(t):
        @pl.when(swapped)
        def _():
            wait_for(frames_in.at[t], fin_sem.at[1, t])
            place(frames_in, t)

        rims(DELTAS, xin.at[t], fcol.at[t], fcor.at[t], xin.at[t], xcin.at[t], sec, fs_sem.at[t], x_sem.at[t])

    @pl.when(first)
    def _():
        enter(0)

    for copy in copies[0::2]:
        copy.wait()

    def spread(buf, t, width, win, base, stride):
        whole = buf[t, 0:NEAR].reshape(NEAR * TC, width)
        for side in range(2):
            moved = jnp.dot(pick[side], whole, preferred_element_type=F32).astype(BF)
            win[TC : TC + PIX, pl.ds(2 * side * stride + base, width)] = moved
        win[TC : TC + PIX, pl.ds(stride + base, width)] = whole[:PIX]

    def spread_far(low, buf, cor, t, width, win, base, stride):
        whole = buf[t, NEAR + low]
        q_at = lax.broadcasted_iota(jnp.int32, (TC, width), 0)
        for side in range(2):
            moved = jnp.dot(pick_far[side], whole, preferred_element_type=F32)
            rim = q_at == (0 if side == 0 else TC - 1)
            cell = jnp.broadcast_to(cor[t, 2 * low + side], (TC, width))
            part = jnp.where(rim, cell, moved)
            win[low * TC : (low + 1) * TC, pl.ds(2 * side * stride + base, width)] = part.astype(BF)
        win[low * TC : (low + 1) * TC, pl.ds(stride + base, width)] = whole

    cells[0] = jnp.zeros((PIX, CH), F32)

    def send_rows(buf, buf_t, dst, dst_t, start, count, section, send_sem, recv_sem):
        pltpu.make_async_remote_copy(
            src_ref=buf.at[buf_t, pl.ds(start, count)],
            dst_ref=dst.at[dst_t, pl.ds(start, count)],
            send_sem=send_sem,
            recv_sem=recv_sem,
            device_id={"section": section, "tile": tile},
            device_id_type=MESH,
        ).start()

    def advance(t, low, high):
        z = z_ref[low:high, :]
        in_gate = jax.nn.sigmoid(z[:, :CH])
        forget = jax.nn.sigmoid(z[:, CH : 2 * CH])
        cand = jnp.tanh(z[:, 2 * CH : 3 * CH])
        out_gate = jax.nn.sigmoid(z[:, 3 * CH :])
        cell = forget * cells[t, low:high, :] + in_gate * cand
        hidden = (out_gate * jnp.tanh(cell)).astype(BF)
        hin[t + 1, low // TC : high // TC] = hidden.reshape((high - low) // TC, TC, CH)
        gates[t, low:high, 0:CH] = in_gate
        gates[t, low:high, CH : 2 * CH] = forget
        gates[t, low:high, 2 * CH : 3 * CH] = cand
        gates[t, low:high, 3 * CH :] = out_gate
        cells[t + 1, low:high, :] = cell
        return hidden.astype(F32)

    def forward(t, carry):
        @pl.when(first & (t < STEPS - 1))
        def _():
            enter(t + 1)

        @pl.when(t > 0)
        def _():
            settle_rims(NEAR_DELTAS, hin.at[t], hcin.at[t], h_sem.at[t])

        spread(hin, t, CH, win_f, CH, 2 * CH)

        @pl.when(sec > 0)
        def _():
            wait_for(xin.at[t, pl.ds(1, TR - 2)], xt_sem.at[t, 0])
            wait_for(xin.at[t, pl.ds(0, 1)], xt_sem.at[t, 1])
            wait_for(xin.at[t, pl.ds(0, 1)], xt_sem.at[t, 2])

        settle_rims(NEAR_DELTAS, xin.at[t], xcin.at[t], x_sem.at[t])
        spread(xin, t, CH, win_f, 0, 2 * CH)
        z = bias_ref[...]
        for a in range(3):
            z = z + lax.dot_general(
                win_f[a * TC : a * TC + PIX, :],
                wf[a],
                (((1,), (1,)), ((), ())),
                preferred_element_type=F32,
            )
        z_ref[...] = z
        advance(t, TC, PIX - TC)

        @pl.when(sec < sections - 1)
        def _():
            send_rows(hin, t + 1, xin, t, 1, TR - 2, sec + 1, xts_sem.at[t, 0], xt_sem.at[t, 0])

        def share(deltas):
            @pl.when(sec < sections - 1)
            def _():
                rims(
                    deltas, hin.at[t + 1], hcol.at[t], hcor.at[t], xin.at[t], xcin.at[t], sec + 1, xs_sem.at[t], x_sem.at[t]
                )

            @pl.when(t < STEPS - 1)
            def _():
                rims(
                    deltas,
                    hin.at[t + 1],
                    hcol.at[t],
                    hcor.at[t],
                    hin.at[t + 1],
                    hcin.at[t + 1],
                    sec,
                    hs_sem.at[t],
                    h_sem.at[t + 1],
                )

        def finish(side):
            deltas = BELOW if side else ABOVE
            start = side * (PIX - TC)

            @pl.when(t > 0)
            def _():
                settle_rims(deltas, hin.at[t], hcin.at[t], h_sem.at[t])

            settle_rims(deltas, xin.at[t], xcin.at[t], x_sem.at[t])
            spread_far(side, hin, hcin, t, CH, far_f, CH, 2 * CH)
            spread_far(side, xin, xcin, t, CH, far_f, 0, 2 * CH)
            z_ref[start : start + TC, :] += lax.dot_general(
                far_f[side * TC : (side + 1) * TC, :],
                wf[2 * side],
                (((1,), (1,)), ((), ())),
                preferred_element_type=F32,
            )
            set_corners(hcor.at[t], side, advance(t, start, start + TC))
            share(ABOVE if side else BELOW)

            @pl.when(sec < sections - 1)
            def _():
                send_rows(hin, t + 1, xin, t, side * (TR - 1), 1, sec + 1, xts_sem.at[t, 1 + side], xt_sem.at[t, 1 + side])

        both_sides(finish)
        field = hin[t + 1, 0:TR].reshape(PIX, CH)
        hcol[t] = columns(field).reshape(2, TR, CH)
        share(NEAR_DELTAS)

        @pl.when(swapped & (t == 0))
        def _():
            to_partner(cot_ref, cot_in, cin_sem.at[0], cin_sem.at[1]).start()

        return carry

    lax.fori_loop(0, STEPS, forward, 0)

    @pl.when(swapped)
    def _():
        wait_for(cot_in, cin_sem.at[1])
        turn_cotangent(cot_in)

    @pl.when(first & kept)
    def _():
        turn_cotangent(cot_ref)

    for copy in copies[1::2]:
        copy.wait()

    def slope(t, low, high):
        in_gate = gates[t, low:high, 0:CH]
        forget = gates[t, low:high, CH : 2 * CH]
        cand = gates[t, low:high, 2 * CH : 3 * CH]
        out_gate = gates[t, low:high, 3 * CH :]
        tanh_cell = jnp.tanh(cells[t + 1, low:high, :])
        rows = (high - low) // TC
        from_above = din[t, low // TC : high // TC].reshape(high - low, CH).astype(F32)
        d_hidden = cot_t[t, low:high, :] + from_above + du_ref[low:high, CH:]
        d_total = dc_ref[low:high, :] + d_hidden * out_gate * (1.0 - tanh_cell * tanh_cell)
        parts = [
            d_total * cand * in_gate * (1.0 - in_gate),
            d_total * cells[t, low:high, :] * forget * (1.0 - forget),
            d_total * in_gate * (1.0 - cand * cand),
            d_hidden * tanh_cell * out_gate * (1.0 - out_gate),
        ]
        dz = jnp.concatenate([part.astype(BF) for part in parts], 1)
        dc_ref[low:high, :] = d_total * forget
        dzin[t, low // TC : high // TC] = dz.reshape(rows, TC, 4 * CH)
        return dz.astype(F32)

    def backward(back, carry):
        t = STEPS - 1 - back

        @pl.when(sec < sections - 1)
        def _():
            wait_for(din.at[t, pl.ds(1, TR - 2)], d_sem.at[t, 0])

        slope(t, TC, PIX - TC)

        def share(deltas):
            rims(
                deltas, dzin.at[t], dzcol.at[t], zcor.at[t], dzin.at[t], zcin.at[t], sec, dzs_sem.at[t], dz_sem.at[t]
            )

        def begin(side):
            start = side * (PIX - TC)

            @pl.when(sec < sections - 1)
            def _():
                wait_for(din.at[t, pl.ds(0, 1)], d_sem.at[t, 1 + side])

            set_corners(zcor.at[t], side, slope(t, start, start + TC))
            share(ABOVE if side else BELOW)

        both_sides(begin)
        dzcol[t] = columns(dzin[t, 0:TR].reshape(PIX, 4 * CH)).reshape(2, TR, 4 * CH)
        share(NEAR_DELTAS)
        emit(0, hidden_ref, t, hin[t + 1, 0:TR])

        @pl.when(back > 0)
        def _():
            emit(1, grads_ref, t + 1, dsend[t + 1])

        settle_rims(NEAR_DELTAS, dzin.at[t], zcin.at[t], dz_sem.at[t])
        spread(dzin, t, 4 * CH, win_b, 0, 4 * CH)
        du = None
        for a in range(3):
            term = jnp.dot(
                win_b[(2 - a) * TC : (2 - a) * TC + PIX, :], wb[a], preferred_element_type=F32
            )
            du = term if du is None else du + term
        du_ref[...] = du
        dsend[t] = du[:, :CH].astype(BF).reshape(TR, TC, CH)
        above = (dsend, t, din, t)

        @pl.when(sec > 0)
        def _():
            send_rows(*above, 1, TR - 2, sec - 1, ds_sem.at[t, 0], d_sem.at[t, 0])

        def finish(side):
            start = side * (PIX - TC)
            settle_rims(BELOW if side else ABOVE, dzin.at[t], zcin.at[t], dz_sem.at[t])
            spread_far(side, dzin, zcin, t, 4 * CH, far_b, 0, 4 * CH)
            rim = du_ref[start : start + TC, :] + jnp.dot(
                far_b[side * TC : (side + 1) * TC, :], wb[2 - 2 * side], preferred_element_type=F32
            )
            du_ref[start : start + TC, :] = rim
            dsend[t, side * (TR - 1)] = rim[:, :CH].astype(BF)

            @pl.when(sec > 0)
            def _():
                send_rows(*above, side * (TR - 1), 1, sec - 1, ds_sem.at[t, 1 + side], d_sem.at[t, 1 + side])

        both_sides(finish)
        return carry

    @pl.when(last)
    def _():
        din[...] = jnp.zeros(din.shape, BF)

    du_ref[...] = jnp.zeros(du_ref.shape, F32)
    dc_ref[...] = jnp.zeros(dc_ref.shape, F32)
    lax.fori_loop(0, STEPS, backward, 0)
    emit(1, grads_ref, 0, dsend[0])

    def settle(t, carry):
        @pl.when(first)
        def _():
            settle_rims(DELTAS, xin.at[t], xcin.at[t], fs_sem.at[t], -1)

        @pl.when(sec < sections - 1)
        def _():
            settle_rims(DELTAS, xin.at[t], xcin.at[t], xs_sem.at[t], -1)
            wait_for(xin.at[t, pl.ds(1, TR - 2)], xts_sem.at[t, 0])
            wait_for(xin.at[t, pl.ds(0, 1)], xts_sem.at[t, 1])
            wait_for(xin.at[t, pl.ds(0, 1)], xts_sem.at[t, 2])

        @pl.when(t < STEPS - 1)
        def _():
            settle_rims(DELTAS, hin.at[t], hcin.at[t], hs_sem.at[t], -1)

        settle_rims(DELTAS, dzin.at[t], zcin.at[t], dzs_sem.at[t], -1)

        @pl.when(sec > 0)
        def _():
            wait_for(dsend.at[t, pl.ds(1, TR - 2)], ds_sem.at[t, 0])
            wait_for(dsend.at[t, pl.ds(0, 1)], ds_sem.at[t, 1])
            wait_for(dsend.at[t, pl.ds(0, 1)], ds_sem.at[t, 2])

        return carry

    lax.fori_loop(0, STEPS, settle, 0)

    @pl.when(first & swapped)
    def _():
        for t in range(STEPS):
            wait_for(frames_in.at[t], fin_sem.at[0, t])

    @pl.when(swapped)
    def _():
        wait_for(cot_in, cin_sem.at[0])

        def fetch(t, carry):
            for which, out_ref in enumerate((hidden_ref, grads_ref)):
                wait_for(stage.at[which, t], out_sem.at[0, which, t])
                wait_for(land.at[which, t], out_sem.at[1, which, t])
                out_ref[t] = land[which, t]
            return carry

        lax.fori_loop(0, STEPS, fetch, 0)


def make_step(sections, tiles):
    def body(*refs):
        kernel(sections, tiles, *refs)

    return pl.pallas_call(
        body,
        out_shape=[jax.ShapeDtypeStruct((STEPS, CH, PIX), BF)] * 2,
        in_specs=[
            pl.BlockSpec(memory_space=pltpu.VMEM),
            pl.BlockSpec(memory_space=pl.ANY),
            pl.BlockSpec(memory_space=pltpu.VMEM),
            pl.BlockSpec(memory_space=pltpu.VMEM),
        ],
        out_specs=[pl.BlockSpec(memory_space=pltpu.VMEM)] * 2,
        scratch_shapes=[
            pltpu.VMEM((STEPS, SLOTS, TC, CH), BF),
            pltpu.VMEM((STEPS + 1, SLOTS, TC, CH), BF),
            pltpu.VMEM((STEPS, SLOTS, TC, 4 * CH), BF),
            pltpu.VMEM((STEPS, TR, TC, CH), BF),
            pltpu.VMEM((STEPS, 2, TR, CH), BF),
            pltpu.VMEM((STEPS, 2, TR, 4 * CH), BF),
            pltpu.VMEM((STEPS, 4, 1, CH), F32),
            pltpu.VMEM((STEPS, 4, 1, CH), F32),
            pltpu.VMEM((STEPS, 4, 1, 4 * CH), F32),
            pltpu.VMEM((STEPS, 4, 1, CH), F32),
            pltpu.VMEM((STEPS, 4, 1, CH), F32),
            pltpu.VMEM((STEPS, 4, 1, 4 * CH), F32),
            pltpu.VMEM((STEPS, CH, PIX), BF),
            pltpu.VMEM((STEPS, CH, PIX), BF),
            pltpu.VMEM((2, STEPS, CH, PIX), BF),
            pltpu.VMEM((2, STEPS, CH, PIX), BF),
            pltpu.VMEM((STEPS, TR, TC, CH), BF),
            pltpu.VMEM((STEPS, 2, TR, CH), BF),
            pltpu.VMEM((3, 4 * CH, 6 * CH), BF),
            pltpu.VMEM((3, 12 * CH, 2 * CH), BF),
            pltpu.VMEM((2, PIX, NEAR * TC), BF),
            pltpu.VMEM((2, TC, TC), BF),
            pltpu.VMEM((2 * TR, PIX), BF),
            pltpu.VMEM((EXT, 6 * CH), BF),
            pltpu.VMEM((EXT, 12 * CH), BF),
            pltpu.VMEM((2 * TC, 6 * CH), BF),
            pltpu.VMEM((2 * TC, 12 * CH), BF),
            pltpu.VMEM((PIX, 4 * CH), F32),
            pltpu.VMEM((PIX, 2 * CH), F32),
            pltpu.VMEM((PIX, CH), F32),
            pltpu.VMEM((STEPS, PIX, 4 * CH), F32),
            pltpu.VMEM((STEPS + 1, PIX, CH), F32),
            pltpu.VMEM((STEPS, PIX, CH), F32),
            pltpu.SemaphoreType.DMA((STEPS, 8)),
            pltpu.SemaphoreType.DMA((STEPS, 8)),
            pltpu.SemaphoreType.DMA((STEPS, 8)),
            pltpu.SemaphoreType.DMA((STEPS, 3)),
            pltpu.SemaphoreType.DMA((STEPS, 3)),
            pltpu.SemaphoreType.DMA((STEPS, 8)),
            pltpu.SemaphoreType.DMA((STEPS, 8)),
            pltpu.SemaphoreType.DMA((STEPS, 8)),
            pltpu.SemaphoreType.DMA((STEPS, 3)),
            pltpu.SemaphoreType.DMA((STEPS, 8)),
            pltpu.SemaphoreType.DMA((STEPS, 3)),
            pltpu.SemaphoreType.DMA((2, 9)),
            pltpu.SemaphoreType.DMA((2, STEPS)),
            pltpu.SemaphoreType.DMA((2,)),
            pltpu.SemaphoreType.DMA((2, 2, STEPS)),
        ],
        compiler_params=pltpu.CompilerParams(
            collective_id=0, has_side_effects=True, vmem_limit_bytes=56 * 1024 * 1024
        ),
        name="conv_lstm",
    )


def solution(mesh):
    step = make_step(mesh.shape["section"], mesh.shape["tile"])

    def per_device(frames, weights, gate_bias, cotangent):
        hidden, grads = step(
            frames.reshape(STEPS, CH, PIX), weights[0], gate_bias, cotangent.reshape(STEPS, CH, PIX)
        )
        shape = (1, STEPS, CH, 1, PIX)
        return hidden.reshape(shape), grads.reshape(shape)

    in_specs = (
        P(None, None, "tile", None),
        P("section", None, None, None),
        P("section", None),
        P("section", None, None, "tile", None),
    )
    out_specs = (P("section", None, None, "tile", None), P("section", None, None, "tile", None))
    return jax.shard_map(
        per_device, mesh=mesh, in_specs=in_specs, out_specs=out_specs, check_vma=False
    )
```
